32 devices in a mesh: grp: 2 (over y), sta: 4 (over z), band: 4 (over x, core), src: 1.
Axes of the slice: x: 2, y: 2, z: 4, core: 2. Of those that a mesh axis runs over, the one named last changes fastest.
Arguments:
- spectra: float32 [1, 192, 1024], P('src', ('grp', 'sta', 'band')), parts along dimension 1, may hold values from -6 to 6
- station_place: int32 [192], P('grp'), parts along dimension 0, may hold values from 0 to 95, each once
- tiles: int32 [32, 2], P(('grp', 'sta', 'band')), parts along dimension 0, may hold values from 0 to 1
- observed: float32 [32, 48, 48, 256], P(('grp', 'sta', 'band')), parts along dimension 0, may hold values from -8 to 8
Outputs:
- adjoint: float32 [1, 192, 1024], P('src', ('grp', 'sta', 'band')), parts along dimension 1
The draws below stay inside these ranges and needn't reach their ends.
There are 2 independent parts, one for each index of `grp`. The reference program is written for one: setup_inputs(seed, part) draws one part's arguments, and reference() takes and returns one part's arrays. A program takes and returns all parts, laid end to end along the dimension named above; each array names one. Nothing has to cross between parts.
Inputs may be any that keep to these rules, and one draw needn't show every extreme that they name: station_place is a permutation; block of station s is station_place[s] // 48.
All inputs are finite; a program needn't handle non-finite values.
Results may differ from the reference program's by a relative error of at most 0.00013.
Values sent between devices are 32-bit elements; how exact they have to be, the bound alone decides.
A program may use at most 64 MiB of HBM per device.

```python
import math
import jax
import jax.numpy as jnp
from jax import lax

TILE = 48
FREQ = 512
LAGS = 256
SRC = 1
STATIONS = 96
BLOCKS = 2
TILES = 16


def touch_ends(array, own_key, smallest, largest):
    longest = array.shape.index(max(array.shape))
    spots = []
    for shift in (0, 1):
        where = [jax.random.randint(jax.random.fold_in(own_key, axis), (), 0, length) for axis, length in enumerate(array.shape)]
        where[longest] = (where[longest] + shift) % array.shape[longest]
        spots.append(tuple(where))
    return array.at[spots[0]].set(smallest).at[spots[1]].set(largest)


def levels(rng, dims, shards, least, high):
    def one(position, parts):
        steps = jax.random.uniform(jax.random.fold_in(jax.random.fold_in(rng, 6), position), (parts,), jnp.float32, least / len(shards), high / len(shards))
        return jnp.repeat(jnp.exp(steps), dims[position] // parts).reshape((-1,) + (1,) * (len(dims) - position - 1))

    gain = one(*shards[0])
    for cut in shards[1:]:
        gain = gain * one(*cut)
    return gain


def noise(stream_key, extent, scale, limit, pieces=(), held_as=jnp.bfloat16):
    drawn = scale * jax.random.normal(stream_key, extent, jnp.float32)
    if pieces:
        drawn = drawn * levels(stream_key, extent, pieces, -0.22, 0.18)
    return jnp.clip(drawn, -limit, limit).astype(held_as)


def setup_inputs(seed: int = 0, part: int = 0) -> dict:
    key_of = jax.random.split(jax.random.key(seed), 5)
    own_keys = jax.random.split(jax.random.fold_in(key_of[4], part), 5)
    spectra = noise(own_keys[0], (SRC, STATIONS, 2 * FREQ), 1.0, 6.0, ((1, 16),), jnp.float32)
    station_place = jax.random.permutation(own_keys[1], STATIONS).astype(jnp.int32)
    tiles = touch_ends(jax.random.randint(own_keys[2], (TILES, 2), 0, BLOCKS), jax.random.fold_in(own_keys[2], 1), 0, BLOCKS - 1).astype(jnp.int32)
    observed = noise(own_keys[3], (TILES, TILE, TILE, LAGS), 2.0, 8.0, ((0, 16),), jnp.float32)
    return {"spectra": spectra, "station_place": station_place, "tiles": tiles, "observed": observed}


cubic_weight = 0.1

def dft_table(freqs, lags):
    fvals = jnp.arange(freqs, dtype=jnp.float32)
    tvals = jnp.arange(lags, dtype=jnp.float32) - lags // 2
    phase = math.pi / freqs * fvals[:, None] * tvals[None, :]
    return jnp.concatenate([jnp.cos(phase), -jnp.sin(phase)], 0) * (1.0 / math.sqrt(freqs))

def cross_spectrum(left, right):
    half = left.shape[-1] // 2
    lre = left[:, :, None, :half]
    lim = left[:, :, None, half:]
    rre = right[:, None, :, :half]
    rim = right[:, None, :, half:]
    real = lax.optimization_barrier(jnp.sum(lre * rre + lim * rim, axis=0))
    imag = lax.optimization_barrier(jnp.sum(lim * rre - lre * rim, axis=0))
    return jnp.concatenate([real, imag], -1)

def adjoint_terms(spectral, left, right):
    half = left.shape[-1] // 2
    are = spectral[:, :, :half]
    aim = spectral[:, :, half:]
    hi = lax.Precision.HIGHEST
    lre, lim = (left[:, :, :half], left[:, :, half:])
    rre, rim = (right[:, :, :half], right[:, :, half:])
    row_re = jnp.einsum('pqf,sqf->spf', are, rre, precision=hi) - jnp.einsum('pqf,sqf->spf', aim, rim, precision=hi)
    row_im = jnp.einsum('pqf,sqf->spf', are, rim, precision=hi) + jnp.einsum('pqf,sqf->spf', aim, rre, precision=hi)
    col_re = jnp.einsum('pqf,spf->sqf', are, lre, precision=hi) + jnp.einsum('pqf,spf->sqf', aim, lim, precision=hi)
    col_im = jnp.einsum('pqf,spf->sqf', are, lim, precision=hi) - jnp.einsum('pqf,spf->sqf', aim, lre, precision=hi)
    rows = jnp.concatenate([row_re, row_im], -1)
    cols = jnp.concatenate([col_re, col_im], -1)
    return jnp.concatenate([rows, cols], 1)

def reference(spectra, station_place, tiles, observed):
    count = station_place.shape[0]
    tile = observed.shape[1]
    lags = observed.shape[3]
    width = spectra.shape[2]
    holder = jnp.zeros((count,), jnp.int32).at[station_place].set(jnp.arange(count, dtype=jnp.int32))
    table = dft_table(width // 2, lags)
    offsets = jnp.arange(tile, dtype=jnp.int32)

    def one_tile(items):
        pair, seen = items
        left = spectra[:, holder[pair[0] * tile + offsets]]
        right = spectra[:, holder[pair[1] * tile + offsets]]
        cross = cross_spectrum(left, right).reshape(tile * tile, width)
        lagged = jnp.dot(cross, table, precision=lax.Precision.HIGHEST, preferred_element_type=jnp.float32)
        misfit = lagged - seen.reshape(tile * tile, lags)
        weighted = misfit + cubic_weight * misfit * misfit * misfit
        spectral = jnp.dot(weighted, table.T, precision=lax.Precision.HIGHEST, preferred_element_type=jnp.float32)
        return adjoint_terms(spectral.reshape(tile, tile, width), left, right)
    terms = lax.map(one_tile, (tiles, observed))
    places = (tiles[:, :, None] * tile + offsets[None, None, :]).reshape(-1)
    targets = holder[places]
    flat = jnp.transpose(terms, (1, 0, 2, 3)).reshape(spectra.shape[0], -1, width)
    total = jnp.zeros(spectra.shape, jnp.float32).at[:, targets].add(flat)
    return total * (1.0 / tile)
```

```python
import functools
import math

import jax
import jax.numpy as jnp
import numpy as np
from jax import lax
from jax.experimental import pallas as pl
from jax.experimental.pallas import tpu as pltpu
from jax.sharding import PartitionSpec as P

cubic_weight = 0.1
LANES = 128
MESH = pl.DeviceIdType.MESH


def dft_table(freqs, lags):
    fvals = jnp.arange(freqs, dtype=jnp.float32)
    tvals = jnp.arange(lags, dtype=jnp.float32) - lags // 2
    phase = math.pi / freqs * fvals[:, None] * tvals[None, :]
    return jnp.concatenate([jnp.cos(phase), -jnp.sin(phase)], 0) * (1.0 / math.sqrt(freqs))


def cross_spectrum(left, right):
    half = left.shape[-1] // 2
    lre = left[:, :, None, :half]
    lim = left[:, :, None, half:]
    rre = right[:, None, :, :half]
    rim = right[:, None, :, half:]
    real = jnp.sum(lre * rre + lim * rim, axis=0)
    imag = jnp.sum(lim * rre - lre * rim, axis=0)
    return jnp.concatenate([real, imag], -1)


def adjoint_terms(spectral, left, right):
    half = left.shape[-1] // 2
    are = spectral[:, :, :half]
    aim = spectral[:, :, half:]
    highest = lax.Precision.HIGHEST
    lre, lim = (left[:, :, :half], left[:, :, half:])
    rre, rim = (right[:, :, :half], right[:, :, half:])
    row_re = jnp.einsum("pqf,sqf->spf", are, rre, precision=highest) - jnp.einsum(
        "pqf,sqf->spf", aim, rim, precision=highest
    )
    row_im = jnp.einsum("pqf,sqf->spf", are, rim, precision=highest) + jnp.einsum(
        "pqf,sqf->spf", aim, rre, precision=highest
    )
    col_re = jnp.einsum("pqf,spf->sqf", are, lre, precision=highest) + jnp.einsum(
        "pqf,spf->sqf", aim, lim, precision=highest
    )
    col_im = jnp.einsum("pqf,spf->sqf", are, lim, precision=highest) - jnp.einsum(
        "pqf,spf->sqf", aim, lre, precision=highest
    )
    rows = jnp.concatenate([row_re, row_im], -1)
    cols = jnp.concatenate([col_re, col_im], -1)
    return jnp.concatenate([rows, cols], 1)


def local(spectra, station_place, tiles, observed):
    tile = observed.shape[1]
    lags = observed.shape[3]
    width = spectra.shape[2]
    slots = tiles.shape[0]
    count = station_place.shape[0]
    table = dft_table(width // 2, lags)
    highest = lax.Precision.HIGHEST
    whole = lax.all_gather(spectra[0], ("sta", "band"), axis=0, tiled=True)
    holder = (
        jnp.zeros((count,), jnp.int32).at[station_place].set(jnp.arange(count, dtype=jnp.int32))
    )
    offsets = jnp.arange(tile, dtype=jnp.int32)
    wanted = (tiles[:, :, None] * tile + offsets[None, None, :]).reshape(-1)
    fetched = jnp.take(whole, holder[wanted], axis=0).reshape(slots, 2, tile, width)
    slot = 0
    cross = cross_spectrum(fetched[slot, 0][None], fetched[slot, 1][None]).reshape(
        tile * tile, width
    )
    partial_lags = [jnp.dot(cross, table, precision=highest, preferred_element_type=jnp.float32)]
    lagged = lax.psum(jnp.stack(partial_lags, 0), "src")
    slot = 0
    misfit = lagged[slot] - observed[slot].reshape(tile * tile, lags)
    weighted = misfit + cubic_weight * misfit * misfit * misfit
    spectral = jnp.dot(weighted, table.T, precision=highest, preferred_element_type=jnp.float32)
    terms = adjoint_terms(
        spectral.reshape(tile, tile, width), fetched[slot, 0][None], fetched[slot, 1][None]
    )
    pieces = terms[0]
    select = (station_place[:, None] == wanted[None, :]).astype(jnp.float32)
    mine = lax.psum_scatter(
        jnp.dot(select, pieces, precision=highest, preferred_element_type=jnp.float32),
        ("sta", "band"),
        scatter_dimension=0,
        tiled=True,
    )
    return (mine * (1.0 / tile))[None]

def tables(freqs, lags, lanes):
    fvals = np.arange(freqs, dtype=np.float64)
    tvals = np.arange(lags // 2, dtype=np.float64) + 0.5
    phase = math.pi / freqs * fvals[:, None] * tvals[None, :]
    scale = 1.0 / math.sqrt(freqs)
    chunks = freqs // lanes
    table = np.stack([np.cos(phase), np.sin(phase)], 0) * scale
    table = table.reshape(2, chunks, lanes, lags // 2).transpose(1, 0, 2, 3)

    def halves(part):
        part = part.astype(np.float32)
        high = part.astype(jnp.bfloat16)
        low = (part - high.astype(np.float32)).astype(jnp.bfloat16)
        return np.concatenate([high, low], -1)

    turn = math.pi / (2 * freqs) * fvals.reshape(chunks, 1, lanes)
    turn = np.concatenate([np.cos(turn), np.sin(turn)], 1).astype(np.float32)
    return halves(table), halves(2.0 * table.transpose(0, 1, 3, 2)), turn


def residue(value):
    return value - value.astype(jnp.bfloat16).astype(jnp.float32)


def fold(value):
    total = value[:8]
    for at in range(8, value.shape[0], 8):
        total = total + value[at:at + 8]
    return total


def halved(acc, lanes):
    got = pltpu.matmul_pop(acc)
    return got[:, :lanes] + got[:, lanes:]


def fused(mesh_sizes, dims, pair_ref, place_ref, turn_ref, spectra_hbm, observed_hbm, down_hbm, up_hbm, out_ref,
          gath, seen, down, up, lag, weights, left, right, rturn, fold_re, fold_im, sendbuf, halfbuf, sumbuf, recvbuf,
          load_sem, table_sem, g1send, g1recv, g2send, g2recv, s1send, s1recv, s2send, s2recv):
    n_sta, n_band = mesh_sizes
    tile, rows, pad, lanes, chunks, block = dims
    n = n_sta * n_band
    pairs = n // 2
    me = lax.axis_index("sta") * n_band + lax.axis_index("band")
    mine, core = me // 2, lax.rem(me, 2)
    real_rows = pl.ds(0, rows)

    def device(pair, side):
        peer = pair * 2 + side
        return {"sta": peer // n_band, "band": lax.rem(peer, n_band)}

    def other(k):
        return lax.rem(mine + k, pairs)

    own = [
        pltpu.make_async_copy(
            spectra_hbm.at[r, pl.ds(h * chunks, chunks), :],
            gath.at[pl.ds(0, chunks), core, mine, r, pl.ds(h * lanes, lanes)],
            load_sem.at[r, h],
        )
        for r in range(rows) for h in range(2)
    ]
    for load in own:
        load.start()
    loads = [
        pltpu.make_async_copy(down_hbm, down, table_sem.at[0]),
        pltpu.make_async_copy(observed_hbm, seen, table_sem.at[1]),
        pltpu.make_async_copy(up_hbm, up, table_sem.at[2]),
    ]
    for load in loads:
        load.start()

    barrier = pltpu.get_barrier_semaphore()

    @pl.loop(1, pairs)
    def _(k):
        pl.semaphore_signal(barrier, inc=1, device_id=device(other(k), core), device_id_type=MESH)

    pl.semaphore_signal(barrier, inc=1, device_id=device(mine, 1 - core), device_id_type=MESH)
    pl.semaphore_wait(barrier, pairs)

    def remote(src, dst, send, recv, pair, side):
        return pltpu.make_async_remote_copy(
            src_ref=src, dst_ref=dst, send_sem=send, recv_sem=recv,
            device_id=device(pair, side), device_id_type=MESH,
        )

    def spread(c, k, holder):
        part = gath.at[c, core, holder, real_rows, :]
        return remote(part, part, g1send.at[c, k], g1recv.at[c, k], other(k), core)

    def forward(c, side):
        part = gath.at[c, side, :, real_rows, :]
        return remote(part, part, g2send.at[c], g2recv.at[c], mine, 1 - core)

    def relay(c):
        @pl.loop(1, pairs)
        def _(k):
            spread(c, k, lax.rem(mine + pairs - k, pairs)).wait_recv()

        forward(c, core).start()

    for load in own:
        load.wait()
    for c in range(chunks):
        @pl.loop(1, pairs)
        def _(k):
            spread(c, k, mine).start()

    count = n * rows
    f32 = jnp.float32
    g_idx = lax.broadcasted_iota(jnp.int32, (8, n * pad), 1)
    slot = g_idx // pad
    holder = slot % pairs * 2 + slot // pairs
    taken = g_idx % pad
    source = jnp.minimum(holder * rows + taken, count - 1)
    places = jnp.concatenate([place_ref[...].astype(f32), jnp.zeros((1, n * pad - count), f32)], -1)
    places = jnp.take_along_axis(jnp.broadcast_to(places, (8, n * pad)), source, axis=1)
    places = jnp.where(taken < rows, places, -1.0)
    places = jnp.broadcast_to(places[0:1, :], (2 * tile, n * pad))
    j_idx = lax.broadcasted_iota(jnp.int32, (2 * tile, n * pad), 0)
    wanted = jnp.where(j_idx < tile, pair_ref[0, 0] * tile + j_idx, pair_ref[0, 1] * tile + j_idx - tile)
    select32 = (jnp.abs(places - wanted.astype(f32)) < 0.5).astype(f32)
    select = jnp.concatenate([select32, select32], -1).astype(jnp.bfloat16)
    back = jnp.transpose(jnp.concatenate([select32, jnp.zeros((n * pad - 2 * tile, n * pad), f32)], 0))
    back = jnp.concatenate([back, back], -1).astype(jnp.bfloat16)
    valid = lax.broadcasted_iota(jnp.int32, (n * pad, 2 * lanes), 0) % pad < rows
    flip = lanes - 1 - lax.broadcasted_iota(jnp.int32, (tile, lanes), 1)
    half = lanes

    def rows_of(p):
        return pl.ds(p * tile, tile)

    loads[1].wait()
    for p in range(tile):
        before = jnp.take_along_axis(seen[rows_of(p), :half], flip, axis=1)
        after = seen[rows_of(p), half:]
        lag[rows_of(p), :half] = -0.5 * (before + after)
        lag[rows_of(p), half:] = 0.5 * (after - before)

    relay(0)
    loads[0].wait()
    def swap(c):
        return remote(
            sendbuf.at[c, 1 - core, :, real_rows, :], halfbuf.at[c, :, real_rows, :],
            s1send.at[c], s1recv.at[c], mine, 1 - core,
        )

    def deliver(c, k):
        return remote(
            sumbuf.at[c, other(k), real_rows, :], recvbuf.at[c, k, real_rows, :],
            s2send.at[c, k], s2recv.at[c, k], other(k), core,
        )

    def combine(c):
        swap(c).wait_recv()
        sumbuf[c] = sendbuf[c, core] + halfbuf[c]

        @pl.loop(1, pairs)
        def _(k):
            deliver(c, k).start()

    delay, slots = 8, 10

    def compute(*accs):
        even, odd, spare, wide = accs[:slots], accs[slots:2 * slots], accs[2 * slots], accs[2 * slots + 1]

        def doubled(part):
            return jnp.concatenate([part, part], 0)

        def prepare(c):
            whole = jnp.where(valid, gath[c].reshape(n * pad, 2 * lanes), 0.0)
            pltpu.matmul_push_rhs(jnp.concatenate([whole, residue(whole)], 0), 0, 0)
            pltpu.matmul_acc_lhs(spare, select, 0)
            got = pltpu.matmul_pop(spare)
            wc, ws = turn_ref[c, 0:1, :], turn_ref[c, 1:2, :]
            lre, lim, rre, rim = got[:tile, :lanes], got[:tile, lanes:], got[tile:, :lanes], got[tile:, lanes:]
            lre, lim = lre * wc + lim * ws, lim * wc - lre * ws
            for k, part in enumerate((lre, lim, lre + lim, lre - lim)):
                left[c, k] = part
            tre, tim = rre * wc - rim * ws, rim * wc + rre * ws
            for k, part in enumerate((tre, tre + tim, tim - tre)):
                rturn[c, k] = part
            for k, part in enumerate((rre, rre + rim, rre - rim)):
                right[k] = part

        def down_step(c, p):
            row = pl.ds(p, 1)
            both = right[0] * left[c, 2, row, :]
            re = both - left[c, 1, row, :] * right[2]
            im = both - left[c, 0, row, :] * right[1]
            load = 0 if p == 0 else None
            pltpu.matmul_acc_lhs(even[p % slots], jnp.concatenate([re, residue(re)], -1), load)
            pltpu.matmul_acc_lhs(odd[p % slots], jnp.concatenate([im, residue(im)], -1), load)

        def down_end(c, p):
            at = rows_of(p)
            e = lag[at, :half] + halved(even[p % slots], lanes)
            o = lag[at, half:] + halved(odd[p % slots], lanes)
            if c < chunks - 1:
                lag[at, :half] = e
                lag[at, half:] = o
            else:
                ee, oo = (2.0 * cubic_weight) * e * e, (2.0 * cubic_weight) * o * o
                base = 1.5 * (ee + oo) + 1.0
                for k, part in enumerate((e * (base - ee), o * (base - oo))):
                    high = part.astype(jnp.bfloat16)
                    weights[k, at, :lanes] = high
                    weights[k, at, lanes:] = (part - high.astype(f32)).astype(jnp.bfloat16)

        for c in range(chunks):
            if c + 1 < chunks:
                relay(c + 1)
            forward(c, 1 - core).wait_recv()
            prepare(c)
            for k in range(2):
                pltpu.matmul_push_rhs(doubled(down[c, k]), 0, k)
            for p in range(tile + delay):
                if p < tile:
                    down_step(c, p)
                if p >= delay:
                    down_end(c, p - delay)

        loads[2].wait()
        for c in range(chunks):
            cols = [None] * 3
            sums = [None, None]

            def add(at, term):
                cols[at] = term if cols[at] is None else cols[at] + term

            def up_step(p):
                load = 0 if p == 0 else None
                pltpu.matmul_acc_lhs(even[p % slots], weights[0, rows_of(p), :], load)
                pltpu.matmul_acc_lhs(odd[p % slots], weights[1, rows_of(p), :], load)

            def up_end(p):
                are = halved(even[p % slots], lanes)
                aim = halved(odd[p % slots], lanes)
                row = pl.ds(p, 1)
                at = pl.ds(p % block * 8, 8)
                both = are + aim
                one = fold(both * rturn[c, 0])
                fold_re[p // block, at, :] = one - fold(aim * rturn[c, 1])
                fold_im[p // block, at, :] = one + fold(are * rturn[c, 2])
                add(0, both * left[c, 1, row, :])
                add(1, are * left[c, 3, row, :])
                add(2, aim * left[c, 2, row, :])

            for k in range(2):
                pltpu.matmul_push_rhs(doubled(up[c, k]), 0, k)
            for p in range(tile + delay):
                if p < tile:
                    up_step(p)
                if p >= delay:
                    up_end(p - delay)
            parts = []
            for part in (fold_re, fold_im):
                blocks = []
                for b in range(tile // block):
                    total = part[b, pl.ds(0, block, stride=8), :]
                    for j in range(1, 8):
                        total = total + part[b, pl.ds(j, block, stride=8), :]
                    blocks.append(total)
                parts.append(jnp.concatenate(blocks, 0))
            terms = jnp.concatenate([
                jnp.concatenate(parts, -1),
                jnp.concatenate([cols[0] + cols[1], cols[0] - cols[2]], -1),
                jnp.zeros((n * pad - 2 * tile, 2 * lanes), f32),
            ], 0)
            pltpu.matmul_push_rhs(jnp.concatenate([terms, residue(terms)], 0), 0, 0)
            pltpu.matmul_acc_lhs(wide, back, 0)
            sendbuf[c] = pltpu.matmul_pop(wide).reshape(2, pairs, pad, 2 * lanes)
            swap(c).start()
            if c > 0:
                combine(c - 1)
        combine(chunks - 1)

    pl.run_scoped(
        compute,
        *[pltpu.ACC(k)((tile, 2 * lanes), f32) for k in (0, 1) for _ in range(slots)],
        pltpu.ACC(0)((2 * tile, 2 * lanes), f32), pltpu.ACC(0)((n * pad, 2 * lanes), f32),
    )

    for c in range(chunks):
        @pl.loop(1, pairs)
        def _(k):
            deliver(c, k).wait_recv()

        total = sumbuf[c, mine]
        for k in range(1, pairs):
            total = total + recvbuf[c, k]
        total = total * (1.0 / tile)
        for h in range(2):
            out_ref[:, h * chunks + c, :] = total[:rows, h * lanes:(h + 1) * lanes]

    for c in range(chunks):
        forward(c, core).wait_send()
        swap(c).wait_send()

        @pl.loop(1, pairs)
        def _(k):
            spread(c, k, mine).wait_send()
            deliver(c, k).wait_send()


def one_kernel(mesh, spectra, station_place, tiles, observed):
    n_sta, n_band = mesh.shape["sta"], mesh.shape["band"]
    n = n_sta * n_band
    tile, lags = observed.shape[1], observed.shape[3]
    rows, width = spectra.shape[1], spectra.shape[2]
    lanes = LANES
    half = width // 2
    chunks = half // lanes
    pad = -(-rows // 8) * 8
    block = 8
    down, up, turn = tables(half, lags, lanes)
    f32, bf16 = jnp.float32, jnp.bfloat16
    dma = pltpu.SemaphoreType.DMA
    anywhere = pl.BlockSpec(memory_space=pl.ANY)
    out = pl.pallas_call(
        functools.partial(fused, (n_sta, n_band), (tile, rows, pad, lanes, chunks, block)),
        out_shape=jax.ShapeDtypeStruct((rows, 2 * chunks, lanes), f32),
        in_specs=[
            pl.BlockSpec(memory_space=pltpu.SMEM), pl.BlockSpec(memory_space=pltpu.VMEM), pl.BlockSpec(memory_space=pltpu.VMEM),
            anywhere, anywhere, anywhere, anywhere,
        ],
        out_specs=pl.BlockSpec(memory_space=pltpu.VMEM),
        scratch_shapes=[
            pltpu.VMEM((chunks, 2, n // 2, pad, 2 * lanes), f32),
            pltpu.VMEM((tile * tile, lags), f32),
            pltpu.VMEM(down.shape, bf16),
            pltpu.VMEM(up.shape, bf16),
            pltpu.VMEM((tile * tile, lags), f32),
            pltpu.VMEM((2, tile * tile, 2 * lanes), bf16),
            pltpu.VMEM((chunks, 4, tile, lanes), f32),
            pltpu.VMEM((3, tile, lanes), f32),
            pltpu.VMEM((chunks, 3, tile, lanes), f32),
            pltpu.VMEM((tile // block, 8 * block, lanes), f32),
            pltpu.VMEM((tile // block, 8 * block, lanes), f32),
            pltpu.VMEM((chunks, 2, n // 2, pad, 2 * lanes), f32),
            pltpu.VMEM((chunks, n // 2, pad, 2 * lanes), f32),
            pltpu.VMEM((chunks, n // 2, pad, 2 * lanes), f32),
            pltpu.VMEM((chunks, n // 2, pad, 2 * lanes), f32),
            dma((rows, 2)), dma((3,)),
            dma((chunks, n // 2)), dma((chunks, n // 2)), dma((chunks,)), dma((chunks,)),
            dma((chunks,)), dma((chunks,)), dma((chunks, n // 2)), dma((chunks, n // 2)),
        ],
        compiler_params=pltpu.CompilerParams(collective_id=0, has_side_effects=True),
        name="adjoint_kernel",
    )(
        tiles, station_place.reshape(1, -1), jnp.asarray(turn), spectra.reshape(rows, 2 * chunks, lanes),
        observed.reshape(tile * tile, lags), jnp.asarray(down), jnp.asarray(up),
    )
    return out.reshape(1, rows, width)


def solution(mesh):
    placed = (
        P("src", ("grp", "sta", "band"), None),
        P("grp"),
        P(("grp", "sta", "band"), None),
        P(("grp", "sta", "band"), None, None, None),
    )
    def body(spectra, station_place, tiles, observed):
        fits = (
            mesh.shape["src"] == 1 and mesh.shape["band"] % 2 == 0 and spectra.shape[0] == 1 and tiles.shape[0] == 1
            and spectra.shape[2] % (2 * LANES) == 0 and observed.shape[1] % 16 == 0
            and observed.shape[3] == 2 * LANES and mesh.shape["sta"] * mesh.shape["band"] == 16 and 2 * observed.shape[1] <= LANES
            and 16 * (-(-spectra.shape[1] // 8) * 8) == LANES
        )
        if fits:
            return one_kernel(mesh, spectra, station_place, tiles, observed)
        return local(spectra, station_place, tiles, observed)

    return jax.shard_map(
        body,
        mesh=mesh,
        in_specs=placed,
        out_specs=P("src", ("grp", "sta", "band"), None),
        check_vma=False,
    )
```

```python
import functools
import math

import jax
import jax.numpy as jnp
import numpy as np
from jax import lax
from jax.experimental import pallas as pl
from jax.experimental.pallas import tpu as pltpu
from jax.sharding import PartitionSpec as P

cubic_weight = 0.1
LANES = 128
MESH = pl.DeviceIdType.MESH


def dft_table(freqs, lags):
    fvals = jnp.arange(freqs, dtype=jnp.float32)
    tvals = jnp.arange(lags, dtype=jnp.float32) - lags // 2
    phase = math.pi / freqs * fvals[:, None] * tvals[None, :]
    return jnp.concatenate([jnp.cos(phase), -jnp.sin(phase)], 0) * (1.0 / math.sqrt(freqs))


def cross_spectrum(left, right):
    half = left.shape[-1] // 2
    lre = left[:, :, None, :half]
    lim = left[:, :, None, half:]
    rre = right[:, None, :, :half]
    rim = right[:, None, :, half:]
    real = jnp.sum(lre * rre + lim * rim, axis=0)
    imag = jnp.sum(lim * rre - lre * rim, axis=0)
    return jnp.concatenate([real, imag], -1)


def adjoint_terms(spectral, left, right):
    half = left.shape[-1] // 2
    are = spectral[:, :, :half]
    aim = spectral[:, :, half:]
    highest = lax.Precision.HIGHEST
    lre, lim = (left[:, :, :half], left[:, :, half:])
    rre, rim = (right[:, :, :half], right[:, :, half:])
    row_re = jnp.einsum("pqf,sqf->spf", are, rre, precision=highest) - jnp.einsum(
        "pqf,sqf->spf", aim, rim, precision=highest
    )
    row_im = jnp.einsum("pqf,sqf->spf", are, rim, precision=highest) + jnp.einsum(
        "pqf,sqf->spf", aim, rre, precision=highest
    )
    col_re = jnp.einsum("pqf,spf->sqf", are, lre, precision=highest) + jnp.einsum(
        "pqf,spf->sqf", aim, lim, precision=highest
    )
    col_im = jnp.einsum("pqf,spf->sqf", are, lim, precision=highest) - jnp.einsum(
        "pqf,spf->sqf", aim, lre, precision=highest
    )
    rows = jnp.concatenate([row_re, row_im], -1)
    cols = jnp.concatenate([col_re, col_im], -1)
    return jnp.concatenate([rows, cols], 1)


def local(spectra, station_place, tiles, observed):
    tile = observed.shape[1]
    lags = observed.shape[3]
    width = spectra.shape[2]
    slots = tiles.shape[0]
    count = station_place.shape[0]
    table = dft_table(width // 2, lags)
    highest = lax.Precision.HIGHEST
    whole = lax.all_gather(spectra[0], ("sta", "band"), axis=0, tiled=True)
    holder = (
        jnp.zeros((count,), jnp.int32).at[station_place].set(jnp.arange(count, dtype=jnp.int32))
    )
    offsets = jnp.arange(tile, dtype=jnp.int32)
    wanted = (tiles[:, :, None] * tile + offsets[None, None, :]).reshape(-1)
    fetched = jnp.take(whole, holder[wanted], axis=0).reshape(slots, 2, tile, width)
    slot = 0
    cross = cross_spectrum(fetched[slot, 0][None], fetched[slot, 1][None]).reshape(
        tile * tile, width
    )
    partial_lags = [jnp.dot(cross, table, precision=highest, preferred_element_type=jnp.float32)]
    lagged = lax.psum(jnp.stack(partial_lags, 0), "src")
    slot = 0
    misfit = lagged[slot] - observed[slot].reshape(tile * tile, lags)
    weighted = misfit + cubic_weight * misfit * misfit * misfit
    spectral = jnp.dot(weighted, table.T, precision=highest, preferred_element_type=jnp.float32)
    terms = adjoint_terms(
        spectral.reshape(tile, tile, width), fetched[slot, 0][None], fetched[slot, 1][None]
    )
    pieces = terms[0]
    select = (station_place[:, None] == wanted[None, :]).astype(jnp.float32)
    mine = lax.psum_scatter(
        jnp.dot(select, pieces, precision=highest, preferred_element_type=jnp.float32),
        ("sta", "band"),
        scatter_dimension=0,
        tiled=True,
    )
    return (mine * (1.0 / tile))[None]

def tables(freqs, lags, lanes):
    fvals = np.arange(freqs, dtype=np.float64)
    tvals = np.arange(lags // 2, dtype=np.float64) + 0.5
    phase = math.pi / freqs * fvals[:, None] * tvals[None, :]
    scale = 1.0 / math.sqrt(freqs)
    chunks = freqs // lanes
    table = np.stack([np.cos(phase), np.sin(phase)], 0) * scale
    table = table.reshape(2, chunks, lanes, lags // 2).transpose(1, 0, 2, 3)

    def halves(part):
        part = part.astype(np.float32)
        high = part.astype(jnp.bfloat16)
        low = (part - high.astype(np.float32)).astype(jnp.bfloat16)
        return np.concatenate([high, low], -1)

    turn = math.pi / (2 * freqs) * fvals.reshape(chunks, 1, lanes)
    turn = np.concatenate([np.cos(turn), np.sin(turn)], 1).astype(np.float32)
    return halves(table), halves(2.0 * table.transpose(0, 1, 3, 2)), turn


def residue(value):
    return value - value.astype(jnp.bfloat16).astype(jnp.float32)


def fold(value):
    total = value[:8]
    for at in range(8, value.shape[0], 8):
        total = total + value[at:at + 8]
    return total


def halved(acc, lanes):
    got = pltpu.matmul_pop(acc)
    return got[:, :lanes] + got[:, lanes:]


def fused(mesh_sizes, dims, pair_hbm, place_hbm, turn_hbm, spectra_hbm, observed_hbm, down_hbm, up_hbm, out_ref,
          pair_ref, place_ref, turn_ref, own, gath, seen, down, up, lag, weights, left, right, rturn, fold_re, fold_im,
          terms, sendbuf, halfbuf, sumbuf, recvbuf,
          load_sem, table_sem, g1send, g1recv, g2send, g2recv, s1send, s1recv, s2send, s2recv):
    n_sta, n_band = mesh_sizes
    tile, rows, pad, lanes, chunks, block = dims
    n = n_sta * n_band
    pairs = n // 2
    me = lax.axis_index("sta") * n_band + lax.axis_index("band")
    mine, core = me // 2, lax.rem(me, 2)
    across = 1 - core
    real_rows = pl.ds(0, rows)
    count = n * rows
    f32 = jnp.float32

    def device(pair, side):
        peer = pair * 2 + side
        return {"sta": peer // n_band, "band": lax.rem(peer, n_band)}

    def other(k):
        return lax.rem(mine + k, pairs)

    barrier = pltpu.get_barrier_semaphore()

    @pl.loop(0, pairs)
    def _(k):
        pl.semaphore_signal(barrier, inc=1, device_id=device(other(k), across), device_id_type=MESH)

    own_loads = [
        pltpu.make_async_copy(
            spectra_hbm.at[:, h * chunks + c, :], own.at[c, real_rows, pl.ds(h * lanes, lanes)], load_sem.at[c, h],
        )
        for c in range(chunks) for h in range(2)
    ]
    for load in own_loads:
        load.start()
    loads = [
        pltpu.make_async_copy(src, dst, table_sem.at[at])
        for at, (src, dst) in enumerate((
            (pair_hbm, pair_ref), (place_hbm, place_ref), (observed_hbm, seen),
            (turn_hbm, turn_ref), (down_hbm, down), (up_hbm, up),
        ))
    ]
    for load in loads:
        load.start()

    def remote(src, dst, send, recv, pair, side):
        return pltpu.make_async_remote_copy(
            src_ref=src, dst_ref=dst, send_sem=send, recv_sem=recv,
            device_id=device(pair, side), device_id_type=MESH,
        )

    def spread(c, k):
        return remote(
            own.at[c, real_rows, :], gath.at[c, core, mine, real_rows, :],
            g1send.at[c], g1recv.at[c], other(k), across,
        )

    def arrived(c):
        part = gath.at[c, across, :, real_rows, :]
        return remote(part, part, g1send.at[c], g1recv.at[c], mine, across)

    def forward(c, side):
        part = gath.at[c, side, :, real_rows, :]
        return remote(part, part, g2send.at[c], g2recv.at[c], mine, across)

    def relay(c):
        arrived(c).wait_recv()
        forward(c, across).start()

    def swap(c):
        return remote(
            sendbuf.at[c, core, :, real_rows, :], halfbuf.at[c, :, real_rows, :],
            s1send.at[c], s1recv.at[c], mine, across,
        )

    def deliver(c, k):
        return remote(
            sumbuf.at[c, other(k), real_rows, :], recvbuf.at[c, k, real_rows, :],
            s2send.at[c], s2recv.at[c], other(k), across,
        )

    def delivered(c):
        part = recvbuf.at[c, :, real_rows, :]
        return remote(part, part, s2send.at[c], s2recv.at[c], mine, across)

    def combine(c):
        swap(c).wait_recv()
        sumbuf[c] = sendbuf[c, across] + halfbuf[c]

        @pl.loop(0, pairs)
        def _(k):
            deliver(c, k).start()

    for load in own_loads:
        load.wait()
    pl.semaphore_wait(barrier, pairs)
    for c in range(chunks):
        @pl.loop(0, pairs)
        def _(k):
            spread(c, k).start()

    for load in loads[:2]:
        load.wait()
    g_idx = lax.broadcasted_iota(jnp.int32, (8, n * pad), 1)
    slot = g_idx // pad
    holder = slot % pairs * 2 + slot // pairs
    taken = g_idx % pad
    source = jnp.minimum(holder * rows + taken, count - 1)
    places = jnp.concatenate([place_ref[...].astype(f32), jnp.zeros((1, n * pad - count), f32)], -1)
    places = jnp.take_along_axis(jnp.broadcast_to(places, (8, n * pad)), source, axis=1)
    places = jnp.where(taken < rows, places, -1.0)
    places = jnp.broadcast_to(places[0:1, :], (2 * tile, n * pad))
    j_idx = lax.broadcasted_iota(jnp.int32, (2 * tile, n * pad), 0)
    wanted = jnp.where(j_idx < tile, pair_ref[0, 0] * tile + j_idx, pair_ref[0, 1] * tile + j_idx - tile)
    select32 = (jnp.abs(places - wanted.astype(f32)) < 0.5).astype(f32)
    select = jnp.concatenate([select32, select32], -1).astype(jnp.bfloat16)
    back = jnp.transpose(jnp.concatenate([select32, jnp.zeros((n * pad - 2 * tile, n * pad), f32)], 0))
    back = jnp.concatenate([back, back], -1).astype(jnp.bfloat16)
    valid = lax.broadcasted_iota(jnp.int32, (n * pad, 2 * lanes), 0) % pad < rows
    flip = lanes - 1 - lax.broadcasted_iota(jnp.int32, (tile, lanes), 1)
    terms[pl.ds(2 * tile, n * pad - 2 * tile), :] = jnp.zeros((n * pad - 2 * tile, 2 * lanes), f32)

    def rows_of(p):
        return pl.ds(p * tile, tile)

    loads[2].wait()
    for p in range(tile):
        before = jnp.take_along_axis(seen[rows_of(p), :lanes], flip, axis=1)
        after = seen[rows_of(p), lanes:]
        lag[rows_of(p), :lanes] = -0.5 * (before + after)
        lag[rows_of(p), lanes:] = 0.5 * (after - before)

    for load in loads[3:]:
        load.wait()
    relay(0)
    delay, slots = 8, 10
    steps = chunks * tile

    def compute(*accs):
        accs, spare, wide = (accs[:slots], accs[slots:2 * slots]), accs[2 * slots], accs[2 * slots + 1]
        fresh = [False, False]

        def stage(unit, value):
            pltpu.matmul_push_rhs(value, 0, unit)
            fresh[unit] = True

        def feed(acc, value, unit):
            pltpu.matmul_acc_lhs(acc, value, 0 if fresh[unit] else None)
            fresh[unit] = False

        def table(ref, c, unit):
            part = ref[c, unit]
            stage(unit, jnp.concatenate([part, part], 0))

        def choose(c):
            forward(c, core).wait_recv()
            whole = jnp.where(valid, gath[c].reshape(n * pad, 2 * lanes), 0.0)
            stage(0, jnp.concatenate([whole, residue(whole)], 0))
            feed(spare, select, 0)

        def prepare(c):
            got = pltpu.matmul_pop(spare)
            wc, ws = turn_ref[c, 0:1, :], turn_ref[c, 1:2, :]
            lre, lim, rre, rim = got[:tile, :lanes], got[:tile, lanes:], got[tile:, :lanes], got[tile:, lanes:]
            lre, lim = lre * wc + lim * ws, lim * wc - lre * ws
            for k, part in enumerate((lre, lim, lre + lim, lre - lim)):
                left[c, k] = part
            tre, tim = rre * wc - rim * ws, rim * wc + rre * ws
            for k, part in enumerate((tre, tre + tim, tim - tre)):
                rturn[c, k] = part
            for k, part in enumerate((rre, rre + rim, rre - rim)):
                right[c % 2, k] = part

        def down_step(i):
            c, p = divmod(i, tile)
            row = pl.ds(p, 1)
            if p == 0:
                for unit in range(2):
                    table(down, c, unit)
            both = right[c % 2, 0] * left[c, 2, row, :]
            re = both - left[c, 1, row, :] * right[c % 2, 2]
            im = both - left[c, 0, row, :] * right[c % 2, 1]
            feed(accs[0][i % slots], jnp.concatenate([re, residue(re)], -1), 0)
            feed(accs[1][i % slots], jnp.concatenate([im, residue(im)], -1), 1)

        def down_end(i):
            c, p = divmod(i, tile)
            at = rows_of(p)
            e = lag[at, :lanes] + halved(accs[0][i % slots], lanes)
            o = lag[at, lanes:] + halved(accs[1][i % slots], lanes)
            if c < chunks - 1:
                lag[at, :lanes] = e
                lag[at, lanes:] = o
            else:
                ee, oo = (2.0 * cubic_weight) * e * e, (2.0 * cubic_weight) * o * o
                base = 1.5 * (ee + oo) + 1.0
                for k, part in enumerate((e * (base - ee), o * (base - oo))):
                    weights[k, at, :lanes] = part
                    weights[k, at, lanes:] = residue(part)

        def run(step, end, hooks):
            for i in range(steps + delay):
                for hook in hooks.pop(i, ()):
                    hook()
                if i < steps:
                    step(i)
                if i >= delay:
                    end(i - delay)
            for i in sorted(hooks):
                for hook in hooks[i]:
                    hook()

        choose(0)
        prepare(0)
        relay(1)
        hooks = {}
        for c in range(1, chunks):
            if c > 1:
                hooks.setdefault((c - 2) * tile + 28, []).append(functools.partial(relay, c))
            hooks.setdefault((c - 1) * tile + 32, []).extend(
                [functools.partial(choose, c), functools.partial(table, down, c - 1, 0)]
            )
            hooks.setdefault((c - 1) * tile + 40, []).append(functools.partial(prepare, c))
        run(down_step, down_end, hooks)

        cols = [None] * 3

        def add(at, term):
            cols[at] = term if cols[at] is None else cols[at] + term

        def up_step(i):
            c, p = divmod(i, tile)
            if p == 0:
                for unit in range(2):
                    table(up, c, unit)
            for unit in range(2):
                feed(accs[unit][i % slots], weights[unit, rows_of(p), :], unit)

        def up_end(i):
            c, p = divmod(i, tile)
            are, aim = [halved(accs[unit][i % slots], lanes) for unit in range(2)]
            row = pl.ds(p, 1)
            at = pl.ds(p % block * 8, 8)
            both = are + aim
            one = fold(both * rturn[c, 0])
            fold_re[p // block, at, :] = one - fold(aim * rturn[c, 1])
            fold_im[p // block, at, :] = one + fold(are * rturn[c, 2])
            add(0, both * left[c, 1, row, :])
            add(1, are * left[c, 3, row, :])
            add(2, aim * left[c, 2, row, :])
            if p % block == block - 1:
                for h, part in enumerate((fold_re, fold_im)):
                    total = part[p // block, pl.ds(0, block, stride=8), :]
                    for j in range(1, 8):
                        total = total + part[p // block, pl.ds(j, block, stride=8), :]
                    terms[pl.ds(p + 1 - block, block), pl.ds(h * lanes, lanes)] = total
            if p == tile - 1:
                terms[pl.ds(tile, tile), :lanes] = cols[0] + cols[1]
                terms[pl.ds(tile, tile), lanes:] = cols[0] - cols[2]
                cols[:] = [None] * 3

        def place(c):
            whole = terms[...]
            stage(0, jnp.concatenate([whole, residue(whole)], 0))
            feed(wide, back, 0)
            if c + 1 < chunks:
                table(up, c + 1, 0)

        def send(c):
            sendbuf[c] = pltpu.matmul_pop(wide).reshape(2, pairs, pad, 2 * lanes)
            swap(c).start()

        hooks = {}
        for c in range(chunks):
            at = (c + 1) * tile + delay
            hooks.setdefault(at, []).append(functools.partial(place, c))
            hooks.setdefault(at + 8, []).append(functools.partial(send, c))
            hooks.setdefault(at + 80, []).append(functools.partial(combine, c))
        run(up_step, up_end, hooks)

    pl.run_scoped(
        compute,
        *[pltpu.ACC(k)((tile, 2 * lanes), f32) for k in (0, 1) for _ in range(slots)],
        pltpu.ACC(0)((2 * tile, 2 * lanes), f32), pltpu.ACC(0)((n * pad, 2 * lanes), f32),
    )

    for c in range(chunks):
        delivered(c).wait_recv()
        total = recvbuf[c, 0]
        for k in range(1, pairs):
            total = total + recvbuf[c, k]
        total = total * (1.0 / tile)
        for h in range(2):
            out_ref[:, h * chunks + c, :] = total[:rows, h * lanes:(h + 1) * lanes]

    for c in range(chunks):
        arrived(c).wait_send()
        forward(c, across).wait_send()
        swap(c).wait_send()
        delivered(c).wait_send()


def one_kernel(mesh, spectra, station_place, tiles, observed):
    n_sta, n_band = mesh.shape["sta"], mesh.shape["band"]
    n = n_sta * n_band
    tile, lags = observed.shape[1], observed.shape[3]
    rows, width = spectra.shape[1], spectra.shape[2]
    lanes = LANES
    half = width // 2
    chunks = half // lanes
    pad = -(-rows // 8) * 8
    block = 8
    down, up, turn = tables(half, lags, lanes)
    f32, bf16 = jnp.float32, jnp.bfloat16
    dma = pltpu.SemaphoreType.DMA
    anywhere = pl.BlockSpec(memory_space=pltpu.HBM)
    out = pl.pallas_call(
        functools.partial(fused, (n_sta, n_band), (tile, rows, pad, lanes, chunks, block)),
        out_shape=jax.ShapeDtypeStruct((rows, 2 * chunks, lanes), f32),
        in_specs=[
            anywhere, anywhere, anywhere, anywhere, anywhere, anywhere, anywhere,
        ],
        out_specs=pl.BlockSpec(memory_space=pltpu.VMEM),
        scratch_shapes=[
            pltpu.SMEM((1, 2), jnp.int32),
            pltpu.VMEM((1, n * rows), jnp.int32),
            pltpu.VMEM(turn.shape, f32),
            pltpu.VMEM((chunks, pad, 2 * lanes), f32),
            pltpu.VMEM((chunks, 2, n // 2, pad, 2 * lanes), f32),
            pltpu.VMEM((tile * tile, lags), f32),
            pltpu.VMEM(down.shape, bf16),
            pltpu.VMEM(up.shape, bf16),
            pltpu.VMEM((tile * tile, lags), f32),
            pltpu.VMEM((2, tile * tile, 2 * lanes), f32),
            pltpu.VMEM((chunks, 4, tile, lanes), f32),
            pltpu.VMEM((2, 3, tile, lanes), f32),
            pltpu.VMEM((chunks, 3, tile, lanes), f32),
            pltpu.VMEM((tile // block, 8 * block, lanes), f32),
            pltpu.VMEM((tile // block, 8 * block, lanes), f32),
            pltpu.VMEM((n * pad, 2 * lanes), f32),
            pltpu.VMEM((chunks, 2, n // 2, pad, 2 * lanes), f32),
            pltpu.VMEM((chunks, n // 2, pad, 2 * lanes), f32),
            pltpu.VMEM((chunks, n // 2, pad, 2 * lanes), f32),
            pltpu.VMEM((chunks, n // 2, pad, 2 * lanes), f32),
            dma((chunks, 2)), dma((6,)), dma((chunks,)), dma((chunks,)), dma((chunks,)), dma((chunks,)),
            dma((chunks,)), dma((chunks,)), dma((chunks,)), dma((chunks,)),
        ],
        compiler_params=pltpu.CompilerParams(collective_id=0, has_side_effects=True),
        name="adjoint_kernel",
    )(
        tiles, station_place.reshape(1, -1), jnp.asarray(turn), spectra.reshape(rows, 2 * chunks, lanes),
        observed.reshape(tile * tile, lags), jnp.asarray(down), jnp.asarray(up),
    )
    return out.reshape(1, rows, width)


def solution(mesh):
    placed = (
        P("src", ("grp", "sta", "band"), None),
        P("grp"),
        P(("grp", "sta", "band"), None),
        P(("grp", "sta", "band"), None, None, None),
    )
    def body(spectra, station_place, tiles, observed):
        fits = (
            mesh.shape["src"] == 1 and mesh.shape["band"] % 2 == 0 and spectra.shape[0] == 1 and tiles.shape[0] == 1
            and spectra.shape[2] % (2 * LANES) == 0 and observed.shape[1] % 16 == 0
            and observed.shape[3] == 2 * LANES and mesh.shape["sta"] * mesh.shape["band"] == 16 and 2 * observed.shape[1] <= LANES
            and 16 * (-(-spectra.shape[1] // 8) * 8) == LANES
        )
        if fits:
            return one_kernel(mesh, spectra, station_place, tiles, observed)
        return local(spectra, station_place, tiles, observed)

    return jax.shard_map(
        body,
        mesh=mesh,
        in_specs=placed,
        out_specs=P("src", ("grp", "sta", "band"), None),
        check_vma=False,
    )
```

```python
import functools
import math

import jax
import jax.numpy as jnp
import numpy as np
from jax import lax
from jax.experimental import pallas as pl
from jax.experimental.pallas import tpu as pltpu
from jax.sharding import PartitionSpec as P

cubic_weight = 0.1
LANES = 128
MESH = pl.DeviceIdType.MESH


def dft_table(freqs, lags):
    fvals = jnp.arange(freqs, dtype=jnp.float32)
    tvals = jnp.arange(lags, dtype=jnp.float32) - lags // 2
    phase = math.pi / freqs * fvals[:, None] * tvals[None, :]
    return jnp.concatenate([jnp.cos(phase), -jnp.sin(phase)], 0) * (1.0 / math.sqrt(freqs))


def cross_spectrum(left, right):
    half = left.shape[-1] // 2
    lre = left[:, :, None, :half]
    lim = left[:, :, None, half:]
    rre = right[:, None, :, :half]
    rim = right[:, None, :, half:]
    real = jnp.sum(lre * rre + lim * rim, axis=0)
    imag = jnp.sum(lim * rre - lre * rim, axis=0)
    return jnp.concatenate([real, imag], -1)


def adjoint_terms(spectral, left, right):
    half = left.shape[-1] // 2
    are = spectral[:, :, :half]
    aim = spectral[:, :, half:]
    highest = lax.Precision.HIGHEST
    lre, lim = (left[:, :, :half], left[:, :, half:])
    rre, rim = (right[:, :, :half], right[:, :, half:])
    row_re = jnp.einsum("pqf,sqf->spf", are, rre, precision=highest) - jnp.einsum(
        "pqf,sqf->spf", aim, rim, precision=highest
    )
    row_im = jnp.einsum("pqf,sqf->spf", are, rim, precision=highest) + jnp.einsum(
        "pqf,sqf->spf", aim, rre, precision=highest
    )
    col_re = jnp.einsum("pqf,spf->sqf", are, lre, precision=highest) + jnp.einsum(
        "pqf,spf->sqf", aim, lim, precision=highest
    )
    col_im = jnp.einsum("pqf,spf->sqf", are, lim, precision=highest) - jnp.einsum(
        "pqf,spf->sqf", aim, lre, precision=highest
    )
    rows = jnp.concatenate([row_re, row_im], -1)
    cols = jnp.concatenate([col_re, col_im], -1)
    return jnp.concatenate([rows, cols], 1)


def local(spectra, station_place, tiles, observed):
    tile = observed.shape[1]
    lags = observed.shape[3]
    width = spectra.shape[2]
    slots = tiles.shape[0]
    count = station_place.shape[0]
    table = dft_table(width // 2, lags)
    highest = lax.Precision.HIGHEST
    whole = lax.all_gather(spectra[0], ("sta", "band"), axis=0, tiled=True)
    holder = (
        jnp.zeros((count,), jnp.int32).at[station_place].set(jnp.arange(count, dtype=jnp.int32))
    )
    offsets = jnp.arange(tile, dtype=jnp.int32)
    wanted = (tiles[:, :, None] * tile + offsets[None, None, :]).reshape(-1)
    fetched = jnp.take(whole, holder[wanted], axis=0).reshape(slots, 2, tile, width)
    slot = 0
    cross = cross_spectrum(fetched[slot, 0][None], fetched[slot, 1][None]).reshape(
        tile * tile, width
    )
    partial_lags = [jnp.dot(cross, table, precision=highest, preferred_element_type=jnp.float32)]
    lagged = lax.psum(jnp.stack(partial_lags, 0), "src")
    slot = 0
    misfit = lagged[slot] - observed[slot].reshape(tile * tile, lags)
    weighted = misfit + cubic_weight * misfit * misfit * misfit
    spectral = jnp.dot(weighted, table.T, precision=highest, preferred_element_type=jnp.float32)
    terms = adjoint_terms(
        spectral.reshape(tile, tile, width), fetched[slot, 0][None], fetched[slot, 1][None]
    )
    pieces = terms[0]
    select = (station_place[:, None] == wanted[None, :]).astype(jnp.float32)
    mine = lax.psum_scatter(
        jnp.dot(select, pieces, precision=highest, preferred_element_type=jnp.float32),
        ("sta", "band"),
        scatter_dimension=0,
        tiled=True,
    )
    return (mine * (1.0 / tile))[None]

def tables(freqs, lags, lanes):
    fvals = np.arange(freqs, dtype=np.float64)
    tvals = np.arange(lags // 2, dtype=np.float64) + 0.5
    phase = math.pi / freqs * fvals[:, None] * tvals[None, :]
    scale = 1.0 / math.sqrt(freqs)
    bend = math.sqrt(2.0 * cubic_weight)
    chunks = freqs // lanes
    table = np.stack([np.cos(phase), np.sin(phase)], 0) * scale
    table = table.reshape(2, chunks, lanes, lags // 2).transpose(1, 0, 2, 3)

    def halves(part):
        part = part.astype(np.float32)
        high = part.astype(jnp.bfloat16)
        low = (part - high.astype(np.float32)).astype(jnp.bfloat16)
        return np.concatenate([high, low], -1)

    turn = math.pi / (2 * freqs) * fvals.reshape(chunks, 1, lanes)
    turn = np.concatenate([np.cos(turn), np.sin(turn)], 1).astype(np.float32)
    return halves(bend * table), halves(2.0 / bend * table.transpose(0, 1, 3, 2)), turn


def residue(value):
    return value - value.astype(jnp.bfloat16).astype(jnp.float32)


def fold(value):
    total = value[:8]
    for at in range(8, value.shape[0], 8):
        total = total + value[at:at + 8]
    return total


def halved(acc, lanes):
    got = pltpu.matmul_pop(acc)
    return got[:, :lanes] + got[:, lanes:]


def fused(mesh_sizes, dims, pair_hbm, place_hbm, turn_hbm, spectra_hbm, observed_hbm, down_hbm, up_hbm, out_ref,
          pair_ref, place_ref, turn_ref, own, gath, seen, down, up, lag, weights, left, right, rturn, fold_re, fold_im,
          terms, sendbuf, halfbuf, sumbuf, recvbuf,
          load_sem, table_sem, g1send, g1recv, g2send, g2recv, s1send, s1recv, s2send, s2recv):
    n_sta, n_band = mesh_sizes
    tile, rows, pad, lanes, chunks, block = dims
    n = n_sta * n_band
    pairs = n // 2
    me = lax.axis_index("sta") * n_band + lax.axis_index("band")
    mine, core = me // 2, lax.rem(me, 2)
    across = 1 - core
    real_rows = pl.ds(0, rows)
    count = n * rows
    f32 = jnp.float32
    bend = math.sqrt(2.0 * cubic_weight)

    def device(pair, side):
        peer = pair * 2 + side
        return {"sta": peer // n_band, "band": lax.rem(peer, n_band)}

    def other(k):
        return lax.rem(mine + k, pairs)

    barrier = pltpu.get_barrier_semaphore()

    @pl.loop(0, pairs)
    def _(k):
        pl.semaphore_signal(barrier, inc=1, device_id=device(other(k), across), device_id_type=MESH)

    own_loads = [
        pltpu.make_async_copy(
            spectra_hbm.at[:, h * chunks + c, :], own.at[c, real_rows, pl.ds(h * lanes, lanes)], load_sem.at[c, h],
        )
        for c in range(chunks) for h in range(2)
    ]
    for load in own_loads:
        load.start()
    loads = [
        pltpu.make_async_copy(src, dst, table_sem.at[at])
        for at, (src, dst) in enumerate((
            (pair_hbm, pair_ref), (place_hbm, place_ref), (observed_hbm, seen),
            (turn_hbm, turn_ref), (down_hbm, down), (up_hbm, up),
        ))
    ]
    for load in loads:
        load.start()

    def remote(src, dst, send, recv, pair, side):
        return pltpu.make_async_remote_copy(
            src_ref=src, dst_ref=dst, send_sem=send, recv_sem=recv,
            device_id=device(pair, side), device_id_type=MESH,
        )

    def spread(c, k):
        return remote(
            own.at[c, real_rows, :], gath.at[c, core, mine, real_rows, :],
            g1send.at[c], g1recv.at[c], other(k), across,
        )

    def arrived(c):
        part = gath.at[c, across, :, real_rows, :]
        return remote(part, part, g1send.at[c], g1recv.at[c], mine, across)

    def forward(c, side):
        part = gath.at[c, side, :, real_rows, :]
        return remote(part, part, g2send.at[c], g2recv.at[c], mine, across)

    def relay(c):
        arrived(c).wait_recv()
        forward(c, across).start()

    def swap(c):
        return remote(
            sendbuf.at[c, core, :, real_rows, :], halfbuf.at[c, :, real_rows, :],
            s1send.at[c], s1recv.at[c], mine, across,
        )

    def deliver(c, k):
        return remote(
            sumbuf.at[c, other(k), real_rows, :], recvbuf.at[c, k, real_rows, :],
            s2send.at[c], s2recv.at[c], other(k), across,
        )

    def delivered(c):
        part = recvbuf.at[c, :, real_rows, :]
        return remote(part, part, s2send.at[c], s2recv.at[c], mine, across)

    def combine(c):
        swap(c).wait_recv()
        sumbuf[c] = sendbuf[c, across] + halfbuf[c]

        @pl.loop(1, pairs + 1)
        def _(k):
            deliver(c, lax.rem(k, pairs)).start()

    for load in own_loads:
        load.wait()
    pl.semaphore_wait(barrier, pairs)
    for c in range(chunks):
        @pl.loop(0, pairs)
        def _(k):
            spread(c, pairs - 1 - k).start()

    for load in loads[:2]:
        load.wait()
    g_idx = lax.broadcasted_iota(jnp.int32, (8, n * pad), 1)
    slot = g_idx // pad
    holder = slot % pairs * 2 + slot // pairs
    taken = g_idx % pad
    source = jnp.minimum(holder * rows + taken, count - 1)
    places = jnp.concatenate([place_ref[...].astype(f32), jnp.zeros((1, n * pad - count), f32)], -1)
    places = jnp.take_along_axis(jnp.broadcast_to(places, (8, n * pad)), source, axis=1)
    places = jnp.where(taken < rows, places, -1.0)
    places = jnp.broadcast_to(places[0:1, :], (2 * tile, n * pad))
    j_idx = lax.broadcasted_iota(jnp.int32, (2 * tile, n * pad), 0)
    wanted = jnp.where(j_idx < tile, pair_ref[0, 0] * tile + j_idx, pair_ref[0, 1] * tile + j_idx - tile)
    select32 = (jnp.abs(places - wanted.astype(f32)) < 0.5).astype(f32)
    select = jnp.concatenate([select32, select32], -1).astype(jnp.bfloat16)
    back = jnp.transpose(jnp.concatenate([select32, jnp.zeros((n * pad - 2 * tile, n * pad), f32)], 0))
    back = jnp.concatenate([back, back], -1).astype(jnp.bfloat16)
    valid = lax.broadcasted_iota(jnp.int32, (n * pad, 2 * lanes), 0) % pad < rows
    flip = lanes - 1 - lax.broadcasted_iota(jnp.int32, (tile, lanes), 1)
    terms[pl.ds(2 * tile, n * pad - 2 * tile), :] = jnp.zeros((n * pad - 2 * tile, 2 * lanes), f32)

    def rows_of(p):
        return pl.ds(pl.multiple_of(p * tile, 8), tile)

    loads[2].wait()
    @pl.loop(0, tile, unroll=4)
    def _(p):
        before = jnp.take_along_axis(seen[rows_of(p), :lanes], flip, axis=1)
        after = seen[rows_of(p), lanes:]
        lag[rows_of(p), :lanes] = -0.5 * bend * (before + after)
        lag[rows_of(p), lanes:] = 0.5 * bend * (after - before)

    for load in loads[3:]:
        load.wait()
    relay(0)
    delay, slots = 9, 12
    steps = chunks * tile

    def compute(*accs):
        accs, spare, wide = (accs[:slots], accs[slots:2 * slots]), accs[2 * slots], accs[2 * slots + 1]
        fresh = [False, False]

        def stage(unit, value):
            pltpu.matmul_push_rhs(value, 0, unit)
            fresh[unit] = True

        def feed(acc, value, unit):
            pltpu.matmul_acc_lhs(acc, value, 0 if fresh[unit] else None)
            fresh[unit] = False

        def table(ref, c, unit):
            part = ref[c, unit]
            stage(unit, jnp.concatenate([part, part], 0))

        def choose(c):
            forward(c, core).wait_recv()
            whole = jnp.where(valid, gath[c].reshape(n * pad, 2 * lanes), 0.0)
            stage(0, jnp.concatenate([whole, residue(whole)], 0))
            feed(spare, select, 0)

        def prepare(c):
            got = pltpu.matmul_pop(spare)
            wc, ws = turn_ref[c, 0:1, :], turn_ref[c, 1:2, :]
            lre, lim, rre, rim = got[:tile, :lanes], got[:tile, lanes:], got[tile:, :lanes], got[tile:, lanes:]
            lre, lim = lre * wc + lim * ws, lim * wc - lre * ws
            for k, part in enumerate((lre, lim, lre + lim, lre - lim)):
                left[c, k] = part
            tre, tim = rre * wc - rim * ws, rim * wc + rre * ws
            for k, part in enumerate((tre, tre + tim, tim - tre)):
                rturn[c, k] = part
            for k, part in enumerate((rre, rre + rim, rre - rim)):
                right[c % 2, k] = part

        def down_step(i):
            c, p = divmod(i, tile)
            row = pl.ds(p, 1)
            if p == 0:
                for unit in range(2):
                    table(down, c, unit)
            both = right[c % 2, 0] * left[c, 2, row, :]
            re = both - left[c, 1, row, :] * right[c % 2, 2]
            im = both - left[c, 0, row, :] * right[c % 2, 1]
            feed(accs[0][i % slots], jnp.concatenate([re, residue(re)], -1), 0)
            feed(accs[1][i % slots], jnp.concatenate([im, residue(im)], -1), 1)

        def down_end(i):
            c, p = divmod(i, tile)
            at = rows_of(p)
            e = lag[at, :lanes] + halved(accs[0][i % slots], lanes)
            o = lag[at, lanes:] + halved(accs[1][i % slots], lanes)
            if c < chunks - 1:
                lag[at, :lanes] = e
                lag[at, lanes:] = o
            else:
                ee, oo = e * e, o * o
                base = 1.5 * (ee + oo) + 1.0
                for k, part in enumerate((e * (base - ee), o * (base - oo))):
                    weights[k, at, :lanes] = part
                    weights[k, at, lanes:] = residue(part)

        def run(step, end, hooks):
            for i in range(steps + delay):
                for hook in hooks.pop(i, ()):
                    hook()
                if i < steps:
                    step(i)
                if i >= delay:
                    end(i - delay)
            for i in sorted(hooks):
                for hook in hooks[i]:
                    hook()

        choose(0)
        prepare(0)
        relay(1)
        hooks = {}
        for c in range(1, chunks):
            if c > 1:
                hooks.setdefault((c - 2) * tile + 28, []).append(functools.partial(relay, c))
            hooks.setdefault((c - 1) * tile + 32, []).extend(
                [functools.partial(choose, c), functools.partial(table, down, c - 1, 0)]
            )
            hooks.setdefault((c - 1) * tile + 40, []).append(functools.partial(prepare, c))
        run(down_step, down_end, hooks)

        cols = [None] * 3

        def add(at, term):
            cols[at] = term if cols[at] is None else cols[at] + term

        def up_step(i):
            c, p = divmod(i, tile)
            if p == 0:
                for unit in range(2):
                    table(up, c, unit)
            for unit in range(2):
                feed(accs[unit][i % slots], weights[unit, rows_of(p), :], unit)

        def up_end(i):
            c, p = divmod(i, tile)
            are, aim = [halved(accs[unit][i % slots], lanes) for unit in range(2)]
            row = pl.ds(p, 1)
            at = pl.ds(p % block * 8, 8)
            both = are + aim
            one = fold(both * rturn[c, 0])
            fold_re[p // block, at, :] = one - fold(aim * rturn[c, 1])
            fold_im[p // block, at, :] = one + fold(are * rturn[c, 2])
            add(0, both * left[c, 1, row, :])
            add(1, are * left[c, 3, row, :])
            add(2, aim * left[c, 2, row, :])
            if p % block == block - 1:
                for h, part in enumerate((fold_re, fold_im)):
                    total = part[p // block, pl.ds(0, block, stride=8), :]
                    for j in range(1, 8):
                        total = total + part[p // block, pl.ds(j, block, stride=8), :]
                    terms[pl.ds(p + 1 - block, block), pl.ds(h * lanes, lanes)] = total
            if p == tile - 1:
                terms[pl.ds(tile, tile), :lanes] = cols[0] + cols[1]
                terms[pl.ds(tile, tile), lanes:] = cols[0] - cols[2]
                cols[:] = [None] * 3

        def place(c):
            whole = terms[...]
            stage(0, jnp.concatenate([whole, residue(whole)], 0))
            feed(wide, back, 0)
            if c + 1 < chunks:
                table(up, c + 1, 0)

        def send(c):
            sendbuf[c] = pltpu.matmul_pop(wide).reshape(2, pairs, pad, 2 * lanes)
            swap(c).start()

        hooks = {}
        for c in range(chunks):
            at = (c + 1) * tile + delay
            hooks.setdefault(at, []).append(functools.partial(place, c))
            hooks.setdefault(at + 8, []).append(functools.partial(send, c))
            hooks.setdefault(at + 80, []).append(functools.partial(combine, c))
        run(up_step, up_end, hooks)

    pl.run_scoped(
        compute,
        *[pltpu.ACC(k)((tile, 2 * lanes), f32) for k in (0, 1) for _ in range(slots)],
        pltpu.ACC(0)((2 * tile, 2 * lanes), f32), pltpu.ACC(0)((n * pad, 2 * lanes), f32),
    )

    for c in range(chunks):
        delivered(c).wait_recv()
        total = recvbuf[c, 0]
        for k in range(1, pairs):
            total = total + recvbuf[c, k]
        total = total * (1.0 / tile)
        for h in range(2):
            out_ref[:, h * chunks + c, :] = total[:rows, h * lanes:(h + 1) * lanes]

    for c in range(chunks):
        arrived(c).wait_send()
        forward(c, across).wait_send()
        swap(c).wait_send()
        delivered(c).wait_send()


def one_kernel(mesh, spectra, station_place, tiles, observed):
    n_sta, n_band = mesh.shape["sta"], mesh.shape["band"]
    n = n_sta * n_band
    tile, lags = observed.shape[1], observed.shape[3]
    rows, width = spectra.shape[1], spectra.shape[2]
    lanes = LANES
    half = width // 2
    chunks = half // lanes
    pad = -(-rows // 8) * 8
    block = 8
    down, up, turn = tables(half, lags, lanes)
    f32, bf16 = jnp.float32, jnp.bfloat16
    dma = pltpu.SemaphoreType.DMA
    anywhere = pl.BlockSpec(memory_space=pltpu.HBM)
    out = pl.pallas_call(
        functools.partial(fused, (n_sta, n_band), (tile, rows, pad, lanes, chunks, block)),
        out_shape=pltpu.VMEM((rows, 2 * chunks, lanes), f32),
        in_specs=[
            anywhere, anywhere, anywhere, anywhere, anywhere, anywhere, anywhere,
        ],
        out_specs=pl.BlockSpec(memory_space=pltpu.VMEM),
        scratch_shapes=[
            pltpu.SMEM((1, 2), jnp.int32),
            pltpu.VMEM((1, n * rows), jnp.int32),
            pltpu.VMEM(turn.shape, f32),
            pltpu.VMEM((chunks, pad, 2 * lanes), f32),
            pltpu.VMEM((chunks, 2, n // 2, pad, 2 * lanes), f32),
            pltpu.VMEM((tile * tile, lags), f32),
            pltpu.VMEM(down.shape, bf16),
            pltpu.VMEM(up.shape, bf16),
            pltpu.VMEM((tile * tile, lags), f32),
            pltpu.VMEM((2, tile * tile, 2 * lanes), f32),
            pltpu.VMEM((chunks, 4, tile, lanes), f32),
            pltpu.VMEM((2, 3, tile, lanes), f32),
            pltpu.VMEM((chunks, 3, tile, lanes), f32),
            pltpu.VMEM((tile // block, 8 * block, lanes), f32),
            pltpu.VMEM((tile // block, 8 * block, lanes), f32),
            pltpu.VMEM((n * pad, 2 * lanes), f32),
            pltpu.VMEM((chunks, 2, n // 2, pad, 2 * lanes), f32),
            pltpu.VMEM((chunks, n // 2, pad, 2 * lanes), f32),
            pltpu.VMEM((chunks, n // 2, pad, 2 * lanes), f32),
            pltpu.VMEM((chunks, n // 2, pad, 2 * lanes), f32),
            dma((chunks, 2)), dma((6,)), dma((chunks,)), dma((chunks,)), dma((chunks,)), dma((chunks,)),
            dma((chunks,)), dma((chunks,)), dma((chunks,)), dma((chunks,)),
        ],
        compiler_params=pltpu.CompilerParams(collective_id=0, has_side_effects=True),
        name="adjoint_kernel",
    )(
        tiles, station_place.reshape(1, -1), jnp.asarray(turn), spectra.reshape(rows, 2 * chunks, lanes),
        observed.reshape(tile * tile, lags), jnp.asarray(down), jnp.asarray(up),
    )
    return out.reshape(1, rows, width)


def solution(mesh):
    placed = (
        P("src", ("grp", "sta", "band"), None),
        P("grp"),
        P(("grp", "sta", "band"), None),
        P(("grp", "sta", "band"), None, None, None),
    )
    def body(spectra, station_place, tiles, observed):
        fits = (
            mesh.shape["src"] == 1 and mesh.shape["band"] % 2 == 0 and spectra.shape[0] == 1 and tiles.shape[0] == 1
            and spectra.shape[2] % (2 * LANES) == 0 and observed.shape[1] % 16 == 0
            and observed.shape[3] == 2 * LANES and mesh.shape["sta"] * mesh.shape["band"] == 16 and 2 * observed.shape[1] <= LANES
            and 16 * (-(-spectra.shape[1] // 8) * 8) == LANES
        )
        if fits:
            return one_kernel(mesh, spectra, station_place, tiles, observed)
        return local(spectra, station_place, tiles, observed)

    return jax.shard_map(
        body,
        mesh=mesh,
        in_specs=placed,
        out_specs=P("src", ("grp", "sta", "band"), None),
        check_vma=False,
    )
```

```python
import functools
import math

import jax
import jax.numpy as jnp
import numpy as np
from jax import lax
from jax.experimental import pallas as pl
from jax.experimental.pallas import tpu as pltpu
from jax.sharding import PartitionSpec as P

cubic_weight = 0.1
LANES = 128
MESH = pl.DeviceIdType.MESH


def dft_table(freqs, lags):
    fvals = jnp.arange(freqs, dtype=jnp.float32)
    tvals = jnp.arange(lags, dtype=jnp.float32) - lags // 2
    phase = math.pi / freqs * fvals[:, None] * tvals[None, :]
    return jnp.concatenate([jnp.cos(phase), -jnp.sin(phase)], 0) * (1.0 / math.sqrt(freqs))


def cross_spectrum(left, right):
    half = left.shape[-1] // 2
    lre = left[:, :, None, :half]
    lim = left[:, :, None, half:]
    rre = right[:, None, :, :half]
    rim = right[:, None, :, half:]
    real = jnp.sum(lre * rre + lim * rim, axis=0)
    imag = jnp.sum(lim * rre - lre * rim, axis=0)
    return jnp.concatenate([real, imag], -1)


def adjoint_terms(spectral, left, right):
    half = left.shape[-1] // 2
    are = spectral[:, :, :half]
    aim = spectral[:, :, half:]
    highest = lax.Precision.HIGHEST
    lre, lim = (left[:, :, :half], left[:, :, half:])
    rre, rim = (right[:, :, :half], right[:, :, half:])
    row_re = jnp.einsum("pqf,sqf->spf", are, rre, precision=highest) - jnp.einsum(
        "pqf,sqf->spf", aim, rim, precision=highest
    )
    row_im = jnp.einsum("pqf,sqf->spf", are, rim, precision=highest) + jnp.einsum(
        "pqf,sqf->spf", aim, rre, precision=highest
    )
    col_re = jnp.einsum("pqf,spf->sqf", are, lre, precision=highest) + jnp.einsum(
        "pqf,spf->sqf", aim, lim, precision=highest
    )
    col_im = jnp.einsum("pqf,spf->sqf", are, lim, precision=highest) - jnp.einsum(
        "pqf,spf->sqf", aim, lre, precision=highest
    )
    rows = jnp.concatenate([row_re, row_im], -1)
    cols = jnp.concatenate([col_re, col_im], -1)
    return jnp.concatenate([rows, cols], 1)


def local(spectra, station_place, tiles, observed):
    tile = observed.shape[1]
    lags = observed.shape[3]
    width = spectra.shape[2]
    slots = tiles.shape[0]
    count = station_place.shape[0]
    table = dft_table(width // 2, lags)
    highest = lax.Precision.HIGHEST
    whole = lax.all_gather(spectra[0], ("sta", "band"), axis=0, tiled=True)
    holder = (
        jnp.zeros((count,), jnp.int32).at[station_place].set(jnp.arange(count, dtype=jnp.int32))
    )
    offsets = jnp.arange(tile, dtype=jnp.int32)
    wanted = (tiles[:, :, None] * tile + offsets[None, None, :]).reshape(-1)
    fetched = jnp.take(whole, holder[wanted], axis=0).reshape(slots, 2, tile, width)
    slot = 0
    cross = cross_spectrum(fetched[slot, 0][None], fetched[slot, 1][None]).reshape(
        tile * tile, width
    )
    partial_lags = [jnp.dot(cross, table, precision=highest, preferred_element_type=jnp.float32)]
    lagged = lax.psum(jnp.stack(partial_lags, 0), "src")
    slot = 0
    misfit = lagged[slot] - observed[slot].reshape(tile * tile, lags)
    weighted = misfit + cubic_weight * misfit * misfit * misfit
    spectral = jnp.dot(weighted, table.T, precision=highest, preferred_element_type=jnp.float32)
    terms = adjoint_terms(
        spectral.reshape(tile, tile, width), fetched[slot, 0][None], fetched[slot, 1][None]
    )
    pieces = terms[0]
    select = (station_place[:, None] == wanted[None, :]).astype(jnp.float32)
    mine = lax.psum_scatter(
        jnp.dot(select, pieces, precision=highest, preferred_element_type=jnp.float32),
        ("sta", "band"),
        scatter_dimension=0,
        tiled=True,
    )
    return (mine * (1.0 / tile))[None]

def tables(freqs, lags, lanes):
    fvals = np.arange(freqs, dtype=np.float64)
    tvals = np.arange(lags // 2, dtype=np.float64) + 0.5
    phase = math.pi / freqs * fvals[:, None] * tvals[None, :]
    scale = 1.0 / math.sqrt(freqs)
    bend = math.sqrt(2.0 * cubic_weight)
    chunks = freqs // lanes
    table = np.stack([np.cos(phase), np.sin(phase)], 0) * scale
    table = table.reshape(2, chunks, lanes, lags // 2).transpose(1, 0, 2, 3)

    def halves(part):
        part = part.astype(np.float32)
        high = part.astype(jnp.bfloat16)
        low = (part - high.astype(np.float32)).astype(jnp.bfloat16)
        return np.concatenate([high, low], -1)

    turn = math.pi / (2 * freqs) * fvals.reshape(chunks, 1, lanes)
    turn = np.concatenate([np.cos(turn), np.sin(turn)], 1).astype(np.float32)
    return halves(bend * table), halves(2.0 / bend * table.transpose(0, 1, 3, 2)), turn


def residue(value):
    return value - value.astype(jnp.bfloat16).astype(jnp.float32)


def fold(value):
    total = value[:8]
    for at in range(8, value.shape[0], 8):
        total = total + value[at:at + 8]
    return total


def halved(acc, lanes):
    got = pltpu.matmul_pop(acc)
    return got[:, :lanes] + got[:, lanes:]


def fused(mesh_sizes, dims, pair_hbm, place_hbm, turn_hbm, spectra_hbm, observed_hbm, down_hbm, up_hbm, out_ref,
          pair_ref, place_ref, turn_ref, own, gath, seen, down, up, lag, weights, left, right, rturn, fold_re, fold_im,
          terms, sendbuf, halfbuf, sumbuf, recvbuf,
          load_sem, table_sem, g1send, g1recv, g2send, g2recv, s1send, s1recv, s2send, s2recv):
    n_sta, n_band = mesh_sizes
    tile, rows, pad, lanes, chunks, block = dims
    n = n_sta * n_band
    pairs = n // 2
    me = lax.axis_index("sta") * n_band + lax.axis_index("band")
    mine, core = me // 2, lax.rem(me, 2)
    across = 1 - core
    real_rows = pl.ds(0, rows)
    count = n * rows
    f32 = jnp.float32
    bend = math.sqrt(2.0 * cubic_weight)

    def device(pair, side):
        peer = pair * 2 + side
        return {"sta": peer // n_band, "band": lax.rem(peer, n_band)}

    def other(k):
        return lax.rem(mine + k, pairs)

    barrier = pltpu.get_barrier_semaphore()

    @pl.loop(0, pairs)
    def _(k):
        pl.semaphore_signal(barrier, inc=1, device_id=device(other(k), across), device_id_type=MESH)

    own_loads = [
        pltpu.make_async_copy(
            spectra_hbm.at[:, h * chunks + c, :], own.at[c, real_rows, pl.ds(h * lanes, lanes)], load_sem.at[c, h],
        )
        for c in range(chunks) for h in range(2)
    ]
    for load in own_loads:
        load.start()
    loads = [
        pltpu.make_async_copy(src, dst, table_sem.at[at])
        for at, (src, dst) in enumerate((
            (pair_hbm, pair_ref), (place_hbm, place_ref), (observed_hbm, seen),
            (turn_hbm, turn_ref), (down_hbm, down), (up_hbm, up),
        ))
    ]
    for load in loads:
        load.start()

    def remote(src, dst, send, recv, pair, side):
        return pltpu.make_async_remote_copy(
            src_ref=src, dst_ref=dst, send_sem=send, recv_sem=recv,
            device_id=device(pair, side), device_id_type=MESH,
        )

    def spread(c, k):
        return remote(
            own.at[c, real_rows, :], gath.at[c, core, mine, real_rows, :],
            g1send.at[c], g1recv.at[c], other(k), across,
        )

    def arrived(c):
        part = gath.at[c, across, :, real_rows, :]
        return remote(part, part, g1send.at[c], g1recv.at[c], mine, across)

    def forward(c, side):
        part = gath.at[c, side, :, real_rows, :]
        return remote(part, part, g2send.at[c], g2recv.at[c], mine, across)

    def relay(c):
        arrived(c).wait_recv()
        forward(c, across).start()

    def swap(c):
        return remote(
            sendbuf.at[c, core, :, real_rows, :], halfbuf.at[c, :, real_rows, :],
            s1send.at[c], s1recv.at[c], mine, across,
        )

    def deliver(c, k):
        return remote(
            sumbuf.at[c, other(k), real_rows, :], recvbuf.at[c, k, real_rows, :],
            s2send.at[c], s2recv.at[c], other(k), across,
        )

    def delivered(c):
        part = recvbuf.at[c, :, real_rows, :]
        return remote(part, part, s2send.at[c], s2recv.at[c], mine, across)

    def combine(c):
        swap(c).wait_recv()
        sumbuf[c] = sendbuf[c, across] + halfbuf[c]

        @pl.loop(1, pairs + 1)
        def _(k):
            deliver(c, lax.rem(k, pairs)).start()

    for load in own_loads:
        load.wait()
    pl.semaphore_wait(barrier, pairs)
    for c in range(chunks):
        @pl.loop(0, pairs)
        def _(k):
            spread(c, pairs - 1 - k).start()

    for load in loads[:2]:
        load.wait()
    g_idx = lax.broadcasted_iota(jnp.int32, (8, n * pad), 1)
    slot = g_idx // pad
    holder = slot % pairs * 2 + slot // pairs
    taken = g_idx % pad
    source = jnp.minimum(holder * rows + taken, count - 1)
    places = jnp.concatenate([place_ref[...].astype(f32), jnp.zeros((1, n * pad - count), f32)], -1)
    places = jnp.take_along_axis(jnp.broadcast_to(places, (8, n * pad)), source, axis=1)
    places = jnp.where(taken < rows, places, -1.0)
    places = jnp.broadcast_to(places[0:1, :], (2 * tile, n * pad))
    j_idx = lax.broadcasted_iota(jnp.int32, (2 * tile, n * pad), 0)
    wanted = jnp.where(j_idx < tile, pair_ref[0, 0] * tile + j_idx, pair_ref[0, 1] * tile + j_idx - tile)
    select32 = (jnp.abs(places - wanted.astype(f32)) < 0.5).astype(f32)
    select = jnp.concatenate([select32, select32], -1).astype(jnp.bfloat16)
    back = jnp.transpose(jnp.concatenate([select32, jnp.zeros((n * pad - 2 * tile, n * pad), f32)], 0))
    back = jnp.concatenate([back, back], -1).astype(jnp.bfloat16)
    valid = lax.broadcasted_iota(jnp.int32, (n * pad, 2 * lanes), 0) % pad < rows
    flip = lanes - 1 - lax.broadcasted_iota(jnp.int32, (tile, lanes), 1)
    terms[pl.ds(2 * tile, n * pad - 2 * tile), :] = jnp.zeros((n * pad - 2 * tile, 2 * lanes), f32)

    def rows_of(p):
        return pl.ds(pl.multiple_of(p * tile, 8), tile)

    loads[2].wait()
    @pl.loop(0, tile, unroll=4)
    def _(p):
        before = jnp.take_along_axis(seen[rows_of(p), :lanes], flip, axis=1)
        after = seen[rows_of(p), lanes:]
        lag[rows_of(p), :lanes] = -0.5 * bend * (before + after)
        lag[rows_of(p), lanes:] = 0.5 * bend * (after - before)

    for load in loads[3:]:
        load.wait()
    relay(0)
    delay, slots = 9, 12
    steps = chunks * tile

    def compute(*accs):
        accs, spare, wide = (accs[:slots], accs[slots:2 * slots]), accs[2 * slots], accs[2 * slots + 1]
        fresh = [False, False]

        def stage(unit, value):
            pltpu.matmul_push_rhs(value, 0, unit)
            fresh[unit] = True

        def feed(acc, value, unit):
            pltpu.matmul_acc_lhs(acc, value, 0 if fresh[unit] else None)
            fresh[unit] = False

        def table(ref, c, unit):
            part = ref[c, unit]
            stage(unit, jnp.concatenate([part, part], 0))

        def choose(c):
            forward(c, core).wait_recv()
            whole = jnp.where(valid, gath[c].reshape(n * pad, 2 * lanes), 0.0)
            stage(0, jnp.concatenate([whole, residue(whole)], 0))
            feed(spare, select, 0)

        def prepare(c):
            got = pltpu.matmul_pop(spare)
            wc, ws = turn_ref[c, 0:1, :], turn_ref[c, 1:2, :]
            lre, lim, rre, rim = got[:tile, :lanes], got[:tile, lanes:], got[tile:, :lanes], got[tile:, lanes:]
            lre, lim = lre * wc + lim * ws, lim * wc - lre * ws
            for k, part in enumerate((lre, lim, lre + lim, lre - lim)):
                left[c, k] = part
            tre, tim = rre * wc - rim * ws, rim * wc + rre * ws
            for k, part in enumerate((tre, tre + tim, tim - tre)):
                rturn[c, k] = part
            for k, part in enumerate((rre, rre + rim, rre - rim)):
                right[c % 2, k] = part

        def down_step(i):
            c, p = divmod(i, tile)
            row = pl.ds(p, 1)
            if p == 0:
                for unit in range(2):
                    table(down, c, unit)
            both = right[c % 2, 0] * left[c, 2, row, :]
            re = both - left[c, 1, row, :] * right[c % 2, 2]
            im = both - left[c, 0, row, :] * right[c % 2, 1]
            feed(accs[0][i % slots], jnp.concatenate([re, residue(re)], -1), 0)
            feed(accs[1][i % slots], jnp.concatenate([im, residue(im)], -1), 1)

        def down_end(i):
            c, p = divmod(i, tile)
            at = rows_of(p)
            e = lag[at, :lanes] + halved(accs[0][i % slots], lanes)
            o = lag[at, lanes:] + halved(accs[1][i % slots], lanes)
            if c < chunks - 1:
                lag[at, :lanes] = e
                lag[at, lanes:] = o
            else:
                ee, oo = e * e, o * o
                base = 1.5 * (ee + oo) + 1.0
                for k, part in enumerate((e * (base - ee), o * (base - oo))):
                    weights[k, at, :lanes] = part
                    weights[k, at, lanes:] = residue(part)

        def run(step, end, hooks):
            for i in range(steps + delay):
                for hook in hooks.pop(i, ()):
                    hook()
                if i < steps:
                    step(i)
                if i >= delay:
                    end(i - delay)
            for i in sorted(hooks):
                for hook in hooks[i]:
                    hook()

        choose(0)
        prepare(0)
        relay(1)
        hooks = {}
        for c in range(1, chunks):
            if c > 1:
                hooks.setdefault((c - 2) * tile + 16, []).append(functools.partial(relay, c))
            hooks.setdefault((c - 1) * tile + 37, []).extend(
                [functools.partial(choose, c), functools.partial(table, down, c - 1, 0)]
            )
            hooks.setdefault((c - 1) * tile + 46, []).append(functools.partial(prepare, c))
        run(down_step, down_end, hooks)

        cols = [None] * 3

        def add(at, term):
            cols[at] = term if cols[at] is None else cols[at] + term

        def up_step(i):
            c, p = divmod(i, tile)
            if p == 0:
                for unit in range(2):
                    table(up, c, unit)
            for unit in range(2):
                feed(accs[unit][i % slots], weights[unit, rows_of(p), :], unit)

        def up_end(i):
            c, p = divmod(i, tile)
            are, aim = [halved(accs[unit][i % slots], lanes) for unit in range(2)]
            row = pl.ds(p, 1)
            at = pl.ds(p % block * 8, 8)
            both = are + aim
            one = fold(both * rturn[c, 0])
            fold_re[p // block, at, :] = one - fold(aim * rturn[c, 1])
            fold_im[p // block, at, :] = one + fold(are * rturn[c, 2])
            add(0, both * left[c, 1, row, :])
            add(1, are * left[c, 3, row, :])
            add(2, aim * left[c, 2, row, :])
            if p % block == block - 1:
                for h, part in enumerate((fold_re, fold_im)):
                    total = part[p // block, pl.ds(0, block, stride=8), :]
                    for j in range(1, 8):
                        total = total + part[p // block, pl.ds(j, block, stride=8), :]
                    terms[pl.ds(p + 1 - block, block), pl.ds(h * lanes, lanes)] = total
            if p == tile - 1:
                terms[pl.ds(tile, tile), :lanes] = cols[0] + cols[1]
                terms[pl.ds(tile, tile), lanes:] = cols[0] - cols[2]
                cols[:] = [None] * 3

        def place(c):
            whole = terms[...]
            stage(0, jnp.concatenate([whole, residue(whole)], 0))
            feed(wide, back, 0)
            if c + 1 < chunks:
                table(up, c + 1, 0)

        def send(c):
            sendbuf[c] = pltpu.matmul_pop(wide).reshape(2, pairs, pad, 2 * lanes)
            swap(c).start()

        hooks = {}
        for c in range(chunks):
            at = (c + 1) * tile + delay
            hooks.setdefault(at, []).append(functools.partial(place, c))
            hooks.setdefault(at + 8, []).append(functools.partial(send, c))
            hooks.setdefault(at + 64, []).append(functools.partial(combine, c))
        run(up_step, up_end, hooks)

    pl.run_scoped(
        compute,
        *[pltpu.ACC(k)((tile, 2 * lanes), f32) for k in (0, 1) for _ in range(slots)],
        pltpu.ACC(0)((2 * tile, 2 * lanes), f32), pltpu.ACC(0)((n * pad, 2 * lanes), f32),
    )

    for c in range(chunks):
        delivered(c).wait_recv()
        total = recvbuf[c, 0]
        for k in range(1, pairs):
            total = total + recvbuf[c, k]
        total = total * (1.0 / tile)
        for h in range(2):
            out_ref[:, h * chunks + c, :] = total[:rows, h * lanes:(h + 1) * lanes]

    for c in range(chunks):
        arrived(c).wait_send()
        forward(c, across).wait_send()
        swap(c).wait_send()
        delivered(c).wait_send()


def one_kernel(mesh, spectra, station_place, tiles, observed):
    n_sta, n_band = mesh.shape["sta"], mesh.shape["band"]
    n = n_sta * n_band
    tile, lags = observed.shape[1], observed.shape[3]
    rows, width = spectra.shape[1], spectra.shape[2]
    lanes = LANES
    half = width // 2
    chunks = half // lanes
    pad = -(-rows // 8) * 8
    block = 8
    down, up, turn = tables(half, lags, lanes)
    f32, bf16 = jnp.float32, jnp.bfloat16
    dma = pltpu.SemaphoreType.DMA
    anywhere = pl.BlockSpec(memory_space=pltpu.HBM)
    out = pl.pallas_call(
        functools.partial(fused, (n_sta, n_band), (tile, rows, pad, lanes, chunks, block)),
        out_shape=pltpu.VMEM((rows, 2 * chunks, lanes), f32),
        in_specs=[
            anywhere, anywhere, anywhere, anywhere, anywhere, anywhere, anywhere,
        ],
        out_specs=pl.BlockSpec(memory_space=pltpu.VMEM),
        scratch_shapes=[
            pltpu.SMEM((1, 2), jnp.int32),
            pltpu.VMEM((1, n * rows), jnp.int32),
            pltpu.VMEM(turn.shape, f32),
            pltpu.VMEM((chunks, pad, 2 * lanes), f32),
            pltpu.VMEM((chunks, 2, n // 2, pad, 2 * lanes), f32),
            pltpu.VMEM((tile * tile, lags), f32),
            pltpu.VMEM(down.shape, bf16),
            pltpu.VMEM(up.shape, bf16),
            pltpu.VMEM((tile * tile, lags), f32),
            pltpu.VMEM((2, tile * tile, 2 * lanes), f32),
            pltpu.VMEM((chunks, 4, tile, lanes), f32),
            pltpu.VMEM((2, 3, tile, lanes), f32),
            pltpu.VMEM((chunks, 3, tile, lanes), f32),
            pltpu.VMEM((tile // block, 8 * block, lanes), f32),
            pltpu.VMEM((tile // block, 8 * block, lanes), f32),
            pltpu.VMEM((n * pad, 2 * lanes), f32),
            pltpu.VMEM((chunks, 2, n // 2, pad, 2 * lanes), f32),
            pltpu.VMEM((chunks, n // 2, pad, 2 * lanes), f32),
            pltpu.VMEM((chunks, n // 2, pad, 2 * lanes), f32),
            pltpu.VMEM((chunks, n // 2, pad, 2 * lanes), f32),
            dma((chunks, 2)), dma((6,)), dma((chunks,)), dma((chunks,)), dma((chunks,)), dma((chunks,)),
            dma((chunks,)), dma((chunks,)), dma((chunks,)), dma((chunks,)),
        ],
        compiler_params=pltpu.CompilerParams(collective_id=0, has_side_effects=True),
        name="adjoint_kernel",
    )(
        tiles, station_place.reshape(1, -1), jnp.asarray(turn), spectra.reshape(rows, 2 * chunks, lanes),
        observed.reshape(tile * tile, lags), jnp.asarray(down), jnp.asarray(up),
    )
    return out.reshape(1, rows, width)


def solution(mesh):
    placed = (
        P("src", ("grp", "sta", "band"), None),
        P("grp"),
        P(("grp", "sta", "band"), None),
        P(("grp", "sta", "band"), None, None, None),
    )
    def body(spectra, station_place, tiles, observed):
        fits = (
            mesh.shape["src"] == 1 and mesh.shape["band"] % 2 == 0 and spectra.shape[0] == 1 and tiles.shape[0] == 1
            and spectra.shape[2] % (2 * LANES) == 0 and observed.shape[1] % 16 == 0
            and observed.shape[3] == 2 * LANES and mesh.shape["sta"] * mesh.shape["band"] == 16 and 2 * observed.shape[1] <= LANES
            and 16 * (-(-spectra.shape[1] // 8) * 8) == LANES
        )
        if fits:
            return one_kernel(mesh, spectra, station_place, tiles, observed)
        return local(spectra, station_place, tiles, observed)

    return jax.shard_map(
        body,
        mesh=mesh,
        in_specs=placed,
        out_specs=P("src", ("grp", "sta", "band"), None),
        check_vma=False,
    )
```

```python
import functools
import math

import jax
import jax.numpy as jnp
import numpy as np
from jax import lax
from jax.experimental import pallas as pl
from jax.experimental.pallas import tpu as pltpu
from jax.sharding import PartitionSpec as P

cubic_weight = 0.1
LANES = 128
MESH = pl.DeviceIdType.MESH


def dft_table(freqs, lags):
    fvals = jnp.arange(freqs, dtype=jnp.float32)
    tvals = jnp.arange(lags, dtype=jnp.float32) - lags // 2
    phase = math.pi / freqs * fvals[:, None] * tvals[None, :]
    return jnp.concatenate([jnp.cos(phase), -jnp.sin(phase)], 0) * (1.0 / math.sqrt(freqs))


def cross_spectrum(left, right):
    half = left.shape[-1] // 2
    lre = left[:, :, None, :half]
    lim = left[:, :, None, half:]
    rre = right[:, None, :, :half]
    rim = right[:, None, :, half:]
    real = jnp.sum(lre * rre + lim * rim, axis=0)
    imag = jnp.sum(lim * rre - lre * rim, axis=0)
    return jnp.concatenate([real, imag], -1)


def adjoint_terms(spectral, left, right):
    half = left.shape[-1] // 2
    are = spectral[:, :, :half]
    aim = spectral[:, :, half:]
    highest = lax.Precision.HIGHEST
    lre, lim = (left[:, :, :half], left[:, :, half:])
    rre, rim = (right[:, :, :half], right[:, :, half:])
    row_re = jnp.einsum("pqf,sqf->spf", are, rre, precision=highest) - jnp.einsum(
        "pqf,sqf->spf", aim, rim, precision=highest
    )
    row_im = jnp.einsum("pqf,sqf->spf", are, rim, precision=highest) + jnp.einsum(
        "pqf,sqf->spf", aim, rre, precision=highest
    )
    col_re = jnp.einsum("pqf,spf->sqf", are, lre, precision=highest) + jnp.einsum(
        "pqf,spf->sqf", aim, lim, precision=highest
    )
    col_im = jnp.einsum("pqf,spf->sqf", are, lim, precision=highest) - jnp.einsum(
        "pqf,spf->sqf", aim, lre, precision=highest
    )
    rows = jnp.concatenate([row_re, row_im], -1)
    cols = jnp.concatenate([col_re, col_im], -1)
    return jnp.concatenate([rows, cols], 1)


def local(spectra, station_place, tiles, observed):
    tile = observed.shape[1]
    lags = observed.shape[3]
    width = spectra.shape[2]
    slots = tiles.shape[0]
    count = station_place.shape[0]
    table = dft_table(width // 2, lags)
    highest = lax.Precision.HIGHEST
    whole = lax.all_gather(spectra[0], ("sta", "band"), axis=0, tiled=True)
    holder = (
        jnp.zeros((count,), jnp.int32).at[station_place].set(jnp.arange(count, dtype=jnp.int32))
    )
    offsets = jnp.arange(tile, dtype=jnp.int32)
    wanted = (tiles[:, :, None] * tile + offsets[None, None, :]).reshape(-1)
    fetched = jnp.take(whole, holder[wanted], axis=0).reshape(slots, 2, tile, width)
    slot = 0
    cross = cross_spectrum(fetched[slot, 0][None], fetched[slot, 1][None]).reshape(
        tile * tile, width
    )
    partial_lags = [jnp.dot(cross, table, precision=highest, preferred_element_type=jnp.float32)]
    lagged = lax.psum(jnp.stack(partial_lags, 0), "src")
    slot = 0
    misfit = lagged[slot] - observed[slot].reshape(tile * tile, lags)
    weighted = misfit + cubic_weight * misfit * misfit * misfit
    spectral = jnp.dot(weighted, table.T, precision=highest, preferred_element_type=jnp.float32)
    terms = adjoint_terms(
        spectral.reshape(tile, tile, width), fetched[slot, 0][None], fetched[slot, 1][None]
    )
    pieces = terms[0]
    select = (station_place[:, None] == wanted[None, :]).astype(jnp.float32)
    mine = lax.psum_scatter(
        jnp.dot(select, pieces, precision=highest, preferred_element_type=jnp.float32),
        ("sta", "band"),
        scatter_dimension=0,
        tiled=True,
    )
    return (mine * (1.0 / tile))[None]

def tables(freqs, lags, lanes):
    fvals = np.arange(freqs, dtype=np.float64)
    tvals = np.arange(lags // 2, dtype=np.float64) + 0.5
    phase = math.pi / freqs * fvals[:, None] * tvals[None, :]
    scale = 1.0 / math.sqrt(freqs)
    bend = math.sqrt(2.0 * cubic_weight)
    chunks = freqs // lanes
    table = np.stack([np.cos(phase), np.sin(phase)], 0) * scale
    table = table.reshape(2, chunks, lanes, lags // 2).transpose(1, 0, 2, 3)

    def halves(part):
        part = part.astype(np.float32)
        high = part.astype(jnp.bfloat16)
        low = (part - high.astype(np.float32)).astype(jnp.bfloat16)
        return np.concatenate([high, low], -1)

    turn = math.pi / (2 * freqs) * fvals.reshape(chunks, 1, lanes)
    turn = np.concatenate([np.cos(turn), np.sin(turn)], 1).astype(np.float32)
    return halves(bend * table), halves(2.0 / bend * table.transpose(0, 1, 3, 2)), turn


def residue(value):
    return value - value.astype(jnp.bfloat16).astype(jnp.float32)


def fold(value):
    total = value[:8]
    for at in range(8, value.shape[0], 8):
        total = total + value[at:at + 8]
    return total


def halved(acc, lanes):
    got = pltpu.matmul_pop(acc)
    return got[:, :lanes] + got[:, lanes:]


def fused(mesh_sizes, dims, pair_hbm, place_hbm, turn_hbm, spectra_hbm, observed_hbm, down_hbm, up_hbm, out_ref,
          pair_ref, place_ref, turn_ref, own, gath, seen, down, up, lag, weights, left, right, rturn, fold_re, fold_im,
          terms, sendbuf, halfbuf, sumbuf, recvbuf,
          load_sem, table_sem, g1send, g1recv, g2send, g2recv, s1send, s1recv, s2send, s2recv):
    n_sta, n_band = mesh_sizes
    tile, rows, pad, lanes, chunks, block = dims
    n = n_sta * n_band
    pairs = n // 2
    me = lax.axis_index("sta") * n_band + lax.axis_index("band")
    mine, core = me // 2, lax.rem(me, 2)
    across = 1 - core
    real_rows = pl.ds(0, rows)
    count = n * rows
    f32 = jnp.float32
    bend = math.sqrt(2.0 * cubic_weight)

    def device(pair, side):
        peer = pair * 2 + side
        return {"sta": peer // n_band, "band": lax.rem(peer, n_band)}

    def other(k):
        return lax.rem(mine + k, pairs)

    barrier = pltpu.get_barrier_semaphore()

    @pl.loop(0, pairs)
    def _(k):
        pl.semaphore_signal(barrier, inc=1, device_id=device(other(k), across), device_id_type=MESH)

    own_loads = [
        pltpu.make_async_copy(
            spectra_hbm.at[:, h * chunks + c, :], own.at[c, real_rows, pl.ds(h * lanes, lanes)], load_sem.at[c, h],
        )
        for c in range(chunks) for h in range(2)
    ]
    for load in own_loads:
        load.start()
    loads = [
        pltpu.make_async_copy(src, dst, table_sem.at[at])
        for at, (src, dst) in enumerate((
            (pair_hbm, pair_ref), (place_hbm, place_ref), (observed_hbm, seen),
            (turn_hbm, turn_ref), (down_hbm, down), (up_hbm, up),
        ))
    ]
    for load in loads:
        load.start()

    def remote(src, dst, send, recv, pair, side):
        return pltpu.make_async_remote_copy(
            src_ref=src, dst_ref=dst, send_sem=send, recv_sem=recv,
            device_id=device(pair, side), device_id_type=MESH,
        )

    def spread(c, k):
        return remote(
            own.at[c, real_rows, :], gath.at[c, core, mine, real_rows, :],
            g1send.at[c], g1recv.at[c], other(k), across,
        )

    def arrived(c):
        part = gath.at[c, across, :, real_rows, :]
        return remote(part, part, g1send.at[c], g1recv.at[c], mine, across)

    def forward(c, side):
        part = gath.at[c, side, :, real_rows, :]
        return remote(part, part, g2send.at[c], g2recv.at[c], mine, across)

    def relay(c):
        arrived(c).wait_recv()
        forward(c, across).start()

    def swap(c):
        return remote(
            sendbuf.at[c, core, :, real_rows, :], halfbuf.at[c, :, real_rows, :],
            s1send.at[c], s1recv.at[c], mine, across,
        )

    def deliver(c, k):
        return remote(
            sumbuf.at[c, other(k), real_rows, :], recvbuf.at[c, k, real_rows, :],
            s2send.at[c], s2recv.at[c], other(k), across,
        )

    def delivered(c):
        part = recvbuf.at[c, :, real_rows, :]
        return remote(part, part, s2send.at[c], s2recv.at[c], mine, across)

    def combine(c):
        swap(c).wait_recv()
        sumbuf[c] = sendbuf[c, across] + halfbuf[c]

        @pl.loop(1, pairs + 1)
        def _(k):
            deliver(c, lax.rem(k, pairs)).start()

    for load in own_loads:
        load.wait()
    pl.semaphore_wait(barrier, pairs)
    for c in range(chunks):
        @pl.loop(0, pairs)
        def _(k):
            spread(c, pairs - 1 - k).start()

    for load in loads[:2]:
        load.wait()
    g_idx = lax.broadcasted_iota(jnp.int32, (8, n * pad), 1)
    slot = g_idx // pad
    holder = slot % pairs * 2 + slot // pairs
    taken = g_idx % pad
    source = jnp.minimum(holder * rows + taken, count - 1)
    places = jnp.concatenate([place_ref[...].astype(f32), jnp.zeros((1, n * pad - count), f32)], -1)
    places = jnp.take_along_axis(jnp.broadcast_to(places, (8, n * pad)), source, axis=1)
    places = jnp.where(taken < rows, places, -1.0)
    places = jnp.broadcast_to(places[0:1, :], (2 * tile, n * pad))
    j_idx = lax.broadcasted_iota(jnp.int32, (2 * tile, n * pad), 0)
    wanted = jnp.where(j_idx < tile, pair_ref[0, 0] * tile + j_idx, pair_ref[0, 1] * tile + j_idx - tile)
    select32 = (jnp.abs(places - wanted.astype(f32)) < 0.5).astype(f32)
    select = jnp.concatenate([select32, select32], -1).astype(jnp.bfloat16)
    back = jnp.transpose(jnp.concatenate([select32, jnp.zeros((n * pad - 2 * tile, n * pad), f32)], 0))
    back = jnp.concatenate([back, back], -1).astype(jnp.bfloat16)
    valid = lax.broadcasted_iota(jnp.int32, (n * pad, 2 * lanes), 0) % pad < rows
    flip = lanes - 1 - lax.broadcasted_iota(jnp.int32, (tile, lanes), 1)
    terms[pl.ds(2 * tile, n * pad - 2 * tile), :] = jnp.zeros((n * pad - 2 * tile, 2 * lanes), f32)

    def rows_of(p):
        return pl.ds(pl.multiple_of(p * tile, 8), tile)

    loads[2].wait()
    @pl.loop(0, tile, unroll=4)
    def _(p):
        before = jnp.take_along_axis(seen[rows_of(p), :lanes], flip, axis=1)
        after = seen[rows_of(p), lanes:]
        lag[rows_of(p), :lanes] = -0.5 * bend * (before + after)
        lag[rows_of(p), lanes:] = 0.5 * bend * (after - before)

    for load in loads[3:]:
        load.wait()
    relay(0)
    delay, slots = 9, 12
    steps = chunks * tile

    def compute(*accs):
        accs, spare, wide = (accs[:slots], accs[slots:2 * slots]), accs[2 * slots], accs[2 * slots + 1]
        fresh = [False, False]

        def stage(unit, value):
            pltpu.matmul_push_rhs(value, 0, unit)
            fresh[unit] = True

        def feed(acc, value, unit):
            pltpu.matmul_acc_lhs(acc, value, 0 if fresh[unit] else None)
            fresh[unit] = False

        def table(ref, c, unit):
            part = ref[c, unit]
            stage(unit, jnp.concatenate([part, part], 0))

        def choose(c):
            forward(c, core).wait_recv()
            whole = jnp.where(valid, gath[c].reshape(n * pad, 2 * lanes), 0.0)
            stage(0, jnp.concatenate([whole, residue(whole)], 0))
            feed(spare, select, 0)

        def prepare(c):
            got = pltpu.matmul_pop(spare)
            wc, ws = turn_ref[c, 0:1, :], turn_ref[c, 1:2, :]
            lre, lim, rre, rim = got[:tile, :lanes], got[:tile, lanes:], got[tile:, :lanes], got[tile:, lanes:]
            lre, lim = lre * wc + lim * ws, lim * wc - lre * ws
            for k, part in enumerate((lre, lim, lre + lim, lre - lim)):
                left[c, k] = part
            tre, tim = rre * wc - rim * ws, rim * wc + rre * ws
            for k, part in enumerate((tre, tre + tim, tim - tre)):
                rturn[c, k] = part
            for k, part in enumerate((rre, rre + rim, rre - rim)):
                right[c % 2, k] = part

        def down_step(i):
            c, p = divmod(i, tile)
            row = pl.ds(p, 1)
            if p == 0:
                for unit in range(2):
                    table(down, c, unit)
            both = right[c % 2, 0] * left[c, 2, row, :]
            re = both - left[c, 1, row, :] * right[c % 2, 2]
            im = both - left[c, 0, row, :] * right[c % 2, 1]
            feed(accs[0][i % slots], jnp.concatenate([re, residue(re)], -1), 0)
            feed(accs[1][i % slots], jnp.concatenate([im, residue(im)], -1), 1)

        def down_end(i):
            c, p = divmod(i, tile)
            at = rows_of(p)
            e = lag[at, :lanes] + halved(accs[0][i % slots], lanes)
            o = lag[at, lanes:] + halved(accs[1][i % slots], lanes)
            if c < chunks - 1:
                lag[at, :lanes] = e
                lag[at, lanes:] = o
            else:
                ee, oo = e * e, o * o
                base = 1.5 * (ee + oo) + 1.0
                for k, part in enumerate((e * (base - ee), o * (base - oo))):
                    weights[k, at, :lanes] = part
                    weights[k, at, lanes:] = residue(part)

        def run(step, end, hooks):
            for i in range(steps + delay):
                for hook in hooks.pop(i, ()):
                    hook()
                if i < steps:
                    step(i)
                if i >= delay:
                    end(i - delay)
            for i in sorted(hooks):
                for hook in hooks[i]:
                    hook()

        choose(0)
        relay(1)
        prepare(0)
        hooks = {}
        for c in range(1, chunks):
            if c > 1:
                hooks.setdefault((c - 2) * tile + 16, []).append(functools.partial(relay, c))
            hooks.setdefault((c - 1) * tile + 37, []).extend(
                [functools.partial(choose, c), functools.partial(table, down, c - 1, 0)]
            )
            hooks.setdefault((c - 1) * tile + 46, []).append(functools.partial(prepare, c))
        run(down_step, down_end, hooks)

        cols = [None] * 3

        def add(at, term):
            cols[at] = term if cols[at] is None else cols[at] + term

        def up_step(i):
            c, p = divmod(i, tile)
            if p == 0:
                for unit in range(2):
                    table(up, c, unit)
            for unit in range(2):
                feed(accs[unit][i % slots], weights[unit, rows_of(p), :], unit)

        def up_end(i):
            c, p = divmod(i, tile)
            are, aim = [halved(accs[unit][i % slots], lanes) for unit in range(2)]
            row = pl.ds(p, 1)
            at = pl.ds(p % block * 8, 8)
            both = are + aim
            one = fold(both * rturn[c, 0])
            fold_re[p // block, at, :] = one - fold(aim * rturn[c, 1])
            fold_im[p // block, at, :] = one + fold(are * rturn[c, 2])
            add(0, both * left[c, 1, row, :])
            add(1, are * left[c, 3, row, :])
            add(2, aim * left[c, 2, row, :])
            if p % block == block - 1:
                for h, part in enumerate((fold_re, fold_im)):
                    total = part[p // block, pl.ds(0, block, stride=8), :]
                    for j in range(1, 8):
                        total = total + part[p // block, pl.ds(j, block, stride=8), :]
                    terms[pl.ds(p + 1 - block, block), pl.ds(h * lanes, lanes)] = total
            if p == tile - 1:
                terms[pl.ds(tile, tile), :lanes] = cols[0] + cols[1]
                terms[pl.ds(tile, tile), lanes:] = cols[0] - cols[2]
                cols[:] = [None] * 3

        def place(c):
            whole = terms[...]
            stage(0, jnp.concatenate([whole, residue(whole)], 0))
            feed(wide, back, 0)
            if c + 1 < chunks:
                table(up, c + 1, 0)

        def send(c):
            sendbuf[c] = pltpu.matmul_pop(wide).reshape(2, pairs, pad, 2 * lanes)
            swap(c).start()

        hooks = {}
        for c in range(chunks):
            at = (c + 1) * tile + delay
            hooks.setdefault(at, []).append(functools.partial(place, c))
            hooks.setdefault(at + 8, []).append(functools.partial(send, c))
            hooks.setdefault(at + 64, []).append(functools.partial(combine, c))
        run(up_step, up_end, hooks)

    pl.run_scoped(
        compute,
        *[pltpu.ACC(k)((tile, 2 * lanes), f32) for k in (0, 1) for _ in range(slots)],
        pltpu.ACC(0)((2 * tile, 2 * lanes), f32), pltpu.ACC(0)((n * pad, 2 * lanes), f32),
    )

    for c in range(chunks):
        delivered(c).wait_recv()
        total = recvbuf[c, 0]
        for k in range(1, pairs):
            total = total + recvbuf[c, k]
        total = total * (1.0 / tile)
        for h in range(2):
            out_ref[:, h * chunks + c, :] = total[:rows, h * lanes:(h + 1) * lanes]

    for c in range(chunks):
        arrived(c).wait_send()
        forward(c, across).wait_send()
        swap(c).wait_send()
        delivered(c).wait_send()


def one_kernel(mesh, spectra, station_place, tiles, observed):
    n_sta, n_band = mesh.shape["sta"], mesh.shape["band"]
    n = n_sta * n_band
    tile, lags = observed.shape[1], observed.shape[3]
    rows, width = spectra.shape[1], spectra.shape[2]
    lanes = LANES
    half = width // 2
    chunks = half // lanes
    pad = -(-rows // 8) * 8
    block = 8
    down, up, turn = tables(half, lags, lanes)
    f32, bf16 = jnp.float32, jnp.bfloat16
    dma = pltpu.SemaphoreType.DMA
    anywhere = pl.BlockSpec(memory_space=pltpu.HBM)
    out = pl.pallas_call(
        functools.partial(fused, (n_sta, n_band), (tile, rows, pad, lanes, chunks, block)),
        out_shape=pltpu.VMEM((rows, 2 * chunks, lanes), f32),
        in_specs=[
            anywhere, anywhere, anywhere, anywhere, anywhere, anywhere, anywhere,
        ],
        out_specs=pl.BlockSpec(memory_space=pltpu.VMEM),
        scratch_shapes=[
            pltpu.SMEM((1, 2), jnp.int32),
            pltpu.VMEM((1, n * rows), jnp.int32),
            pltpu.VMEM(turn.shape, f32),
            pltpu.VMEM((chunks, pad, 2 * lanes), f32),
            pltpu.VMEM((chunks, 2, n // 2, pad, 2 * lanes), f32),
            pltpu.VMEM((tile * tile, lags), f32),
            pltpu.VMEM(down.shape, bf16),
            pltpu.VMEM(up.shape, bf16),
            pltpu.VMEM((tile * tile, lags), f32),
            pltpu.VMEM((2, tile * tile, 2 * lanes), f32),
            pltpu.VMEM((chunks, 4, tile, lanes), f32),
            pltpu.VMEM((2, 3, tile, lanes), f32),
            pltpu.VMEM((chunks, 3, tile, lanes), f32),
            pltpu.VMEM((tile // block, 8 * block, lanes), f32),
            pltpu.VMEM((tile // block, 8 * block, lanes), f32),
            pltpu.VMEM((n * pad, 2 * lanes), f32),
            pltpu.VMEM((chunks, 2, n // 2, pad, 2 * lanes), f32),
            pltpu.VMEM((chunks, n // 2, pad, 2 * lanes), f32),
            pltpu.VMEM((chunks, n // 2, pad, 2 * lanes), f32),
            pltpu.VMEM((chunks, n // 2, pad, 2 * lanes), f32),
            dma((chunks, 2)), dma((6,)), dma((chunks,)), dma((chunks,)), dma((chunks,)), dma((chunks,)),
            dma((chunks,)), dma((chunks,)), dma((chunks,)), dma((chunks,)),
        ],
        compiler_params=pltpu.CompilerParams(collective_id=0, has_side_effects=True),
        name="adjoint_kernel",
    )(
        tiles, station_place.reshape(1, -1), jnp.asarray(turn), spectra.reshape(rows, 2 * chunks, lanes),
        observed.reshape(tile * tile, lags), jnp.asarray(down), jnp.asarray(up),
    )
    return out.reshape(1, rows, width)


def solution(mesh):
    placed = (
        P("src", ("grp", "sta", "band"), None),
        P("grp"),
        P(("grp", "sta", "band"), None),
        P(("grp", "sta", "band"), None, None, None),
    )
    def body(spectra, station_place, tiles, observed):
        fits = (
            mesh.shape["src"] == 1 and mesh.shape["band"] % 2 == 0 and spectra.shape[0] == 1 and tiles.shape[0] == 1
            and spectra.shape[2] % (2 * LANES) == 0 and observed.shape[1] % 16 == 0
            and observed.shape[3] == 2 * LANES and mesh.shape["sta"] * mesh.shape["band"] == 16 and 2 * observed.shape[1] <= LANES
            and 16 * (-(-spectra.shape[1] // 8) * 8) == LANES
        )
        if fits:
            return one_kernel(mesh, spectra, station_place, tiles, observed)
        return local(spectra, station_place, tiles, observed)

    return jax.shard_map(
        body,
        mesh=mesh,
        in_specs=placed,
        out_specs=P("src", ("grp", "sta", "band"), None),
        check_vma=False,
    )
```
